512 devices in a mesh: rows: 16 (over y_lo, x, core), cols: 32 (over y_hi, z).
Axes of the slice: x: 4, y: 4 (y_hi: 2, y_lo: 2; y = y_hi * 2 + y_lo), z: 16, core: 2. Of those that a mesh axis runs over, the one named last changes fastest.
Arguments:
- e_field: float32 [3, 128, 512, 128], P(None, 'rows', 'cols'), may hold values from -6 to 6
- h_field: float32 [3, 128, 512, 128], P(None, 'rows', 'cols'), may hold values from -6 to 6
- polar: float32 [3, 128, 512, 128], P(None, 'rows', 'cols'), may hold values from -4 to 4
- polar_rate: float32 [3, 128, 512, 128], P(None, 'rows', 'cols'), may hold values from -4 to 4
- material_id: int32 [128, 512, 128], P('rows', 'cols'), may hold values from 0 to 7
- eps_inf: float32 [8], replicated, may hold values from 1 to 6
- delta_eps: float32 [8], replicated, may hold values from 0.5 to 4
- pole_freq: float32 [8], replicated, may hold values from 0.1 to 0.6
- damping: float32 [8], replicated, may hold values from 0.02 to 0.3
- dft_acc: float32 [8, 128, 512, 128], P(None, 'rows', 'cols'), may hold values from -6 to 6
- plane_index: int32 [1], replicated, may hold values from 1 to 127
- direction_ids: int32 [256, 2], replicated, may hold values from 0 to 63
Outputs:
- e_out: float32 [3, 128, 512, 128], P(None, 'rows', 'cols')
- h_out: float32 [3, 128, 512, 128], P(None, 'rows', 'cols')
- polar_out: float32 [3, 128, 512, 128], P(None, 'rows', 'cols')
- rate_out: float32 [3, 128, 512, 128], P(None, 'rows', 'cols')
- dft_out: float32 [8, 128, 512, 128], P(None, 'rows', 'cols')
- far_field: float32 [8, 128, 256], P(None, 'rows', 'cols')
The draws below stay inside these ranges and needn't reach their ends.
All inputs are finite; a program needn't handle non-finite values.
Results may differ from the reference program's by a relative error of at most 0.0002.
Values sent between devices are 32-bit elements; how exact they have to be, the bound alone decides.
No kernel may reach another device: no remote copies, remote signals or barrier semaphores. Data moves between devices by JAX's collectives and lax.ppermute only.
A program may use at most 64 MiB of HBM per device.

```python
import math
import jax
import jax.numpy as jnp
from jax import lax

NZ = 128
STEPS = 8
F = 128
D = 256
NMAT = 8
G = 64
NX = 128
NY = 512


def set_ends(array, key, least, top_value):
    longest = array.shape.index(max(array.shape))
    spots = []
    for shift in (0, 1):
        where = [jax.random.randint(jax.random.fold_in(key, axis), (), 0, length) for axis, length in enumerate(array.shape)]
        where[longest] = (where[longest] + shift) % array.shape[longest]
        spots.append(tuple(where))
    return array.at[spots[0]].set(least).at[spots[1]].set(top_value)


def level_of(stream_key, extent, shards, smallest, largest):
    def one(axis_at, shards_of):
        heights = jax.random.uniform(jax.random.fold_in(jax.random.fold_in(stream_key, 6), axis_at), (shards_of,), jnp.float32, smallest / len(shards), largest / len(shards))
        return jnp.repeat(jnp.exp(heights), extent[axis_at] // shards_of).reshape((-1,) + (1,) * (len(extent) - axis_at - 1))

    level = one(*shards[0])
    for cut in shards[1:]:
        level = level * one(*cut)
    return level


def centred(rng, extent, width, most, shards=(), kind=jnp.bfloat16):
    level = level_of(rng, extent, shards, -0.22, 0.18) if shards else 1.0
    array = jax.random.normal(rng, extent, jnp.float32) * width * level
    return jnp.minimum(jnp.maximum(array, -most), most).astype(kind)


def setup_inputs(seed: int = 0) -> dict:
    keys = jax.random.split(jax.random.key(seed), 13)
    return {
        "e_field": centred(keys[0], (3, NX, NY, NZ), 1.0, 6.0, ((1, 16), (2, 32)), jnp.float32),
        "h_field": centred(keys[1], (3, NX, NY, NZ), 1.0, 6.0, ((1, 16), (2, 32)), jnp.float32),
        "polar": centred(keys[2], (3, NX, NY, NZ), 0.5, 4.0, ((1, 16), (2, 32)), jnp.float32),
        "polar_rate": centred(keys[3], (3, NX, NY, NZ), 0.5, 4.0, ((1, 16), (2, 32)), jnp.float32),
        "material_id": set_ends(jax.random.randint(keys[4], (NX, NY, NZ), 0, NMAT), jax.random.fold_in(keys[4], 1), 0, NMAT - 1).astype(jnp.int32),
        "eps_inf": jnp.clip(jnp.exp(jax.random.uniform(keys[5], (NMAT,), jnp.float32, math.log(1.0), math.log(6.0))), 1.0, 6.0),
        "delta_eps": jnp.clip(jnp.exp(jax.random.uniform(keys[6], (NMAT,), jnp.float32, math.log(0.5), math.log(4.0))), 0.5, 4.0),
        "pole_freq": jnp.clip(jnp.exp(jax.random.uniform(keys[7], (NMAT,), jnp.float32, math.log(0.1), math.log(0.6))), 0.1, 0.6),
        "damping": jnp.clip(jnp.exp(jax.random.uniform(keys[8], (NMAT,), jnp.float32, math.log(0.02), math.log(0.3))), 0.02, 0.3),
        "dft_acc": centred(keys[9], (8, F, NY, NZ), 1.0, 6.0, ((1, 16), (2, 32)), jnp.float32),
        "plane_index": jax.random.randint(keys[10], (1,), 1, NX).astype(jnp.int32),
        "direction_ids": set_ends(jax.random.randint(keys[11], (D, 2), 0, G), jax.random.fold_in(keys[11], 1), 0, G - 1).astype(jnp.int32),
    }


COURANT = 0.5
OMEGA_LO = 2.0 * math.pi / 24.0
OMEGA_HI = 2.0 * math.pi / 12.0
SPREAD = 0.7
BEST_PRECISION = lax.Precision.HIGHEST

def next_along(values, axis, rim):
    return jnp.concatenate([lax.slice_in_dim(values, 1, values.shape[axis], axis=axis), rim], axis)

def prev_along(values, axis, rim):
    return jnp.concatenate([rim, lax.slice_in_dim(values, 0, values.shape[axis] - 1, axis=axis)], axis)

def zero_rim(values, axis):
    return jnp.zeros_like(lax.slice_in_dim(values, 0, 1, axis=axis))

def curl_forward(field_in, row_next, col_next):
    elec_x, elec_y, elec_z = (field_in[0], field_in[1], field_in[2])
    y_plus_x = next_along(elec_y, 0, row_next[0])
    z_plus_x = next_along(elec_z, 0, row_next[1])
    x_plus_y = next_along(elec_x, 1, col_next[0])
    z_plus_y = next_along(elec_z, 1, col_next[1])
    x_plus_z = next_along(elec_x, 2, zero_rim(elec_x, 2))
    y_plus_z = next_along(elec_y, 2, zero_rim(elec_y, 2))
    return jnp.stack([z_plus_y - elec_z - (y_plus_z - elec_y), x_plus_z - elec_x - (z_plus_x - elec_z), y_plus_x - elec_y - (x_plus_y - elec_x)])

def curl_backward(field_in, row_prev, col_prev):
    magn_x, magn_y, magn_z = (field_in[0], field_in[1], field_in[2])
    y_minus_x = prev_along(magn_y, 0, row_prev[0])
    z_minus_x = prev_along(magn_z, 0, row_prev[1])
    x_minus_y = prev_along(magn_x, 1, col_prev[0])
    z_minus_y = prev_along(magn_z, 1, col_prev[1])
    x_minus_z = prev_along(magn_x, 2, zero_rim(magn_x, 2))
    y_minus_z = prev_along(magn_y, 2, zero_rim(magn_y, 2))
    return jnp.stack([magn_z - z_minus_y - (magn_y - y_minus_z), magn_x - x_minus_z - (magn_z - z_minus_x), magn_y - y_minus_x - (magn_x - x_minus_y)])

def material_terms(material_id, eps_inf, delta_eps, pole_freq, damping):
    levels = jnp.arange(eps_inf.shape[0], dtype=jnp.int32)
    onehot = (material_id[None] == levels[:, None, None, None]).astype(eps_inf.dtype)

    def lookup(entries):
        return lax.optimization_barrier(jnp.sum(onehot * entries[:, None, None, None], axis=0))
    half_damp = 0.5 * lookup(damping)
    pole = lookup(pole_freq)
    keep_rate = (1.0 - half_damp) / (1.0 + half_damp)
    drive_gain = pole * pole / COURANT / (1.0 + half_damp)
    return (keep_rate, drive_gain, lookup(delta_eps), COURANT / lookup(eps_inf))

def plane_sample(e_field, h_field, plane_row):
    return jnp.concatenate([lax.dynamic_index_in_dim(e_field[1:3], plane_row, 1, keepdims=False), lax.dynamic_index_in_dim(h_field[1:3], plane_row, 1, keepdims=False)], 0)

def frequencies(freq_ids, total):
    return OMEGA_LO + (OMEGA_HI - OMEGA_LO) * (freq_ids.astype(jnp.float32) / (total - 1))

def sample_times(count):
    return (jnp.arange(count).astype(jnp.float32) + 1.0) * COURANT

def update_dft(acc, angles, stacked):
    real_part = acc[:4] + jnp.einsum('nf,ncyz->cfyz', jnp.cos(angles), stacked, precision=BEST_PRECISION)
    imag_part = acc[4:] - jnp.einsum('nf,ncyz->cfyz', jnp.sin(angles), stacked, precision=BEST_PRECISION)
    return jnp.concatenate([real_part, imag_part], 0)

def currents(parts):
    return jnp.stack([-parts[3], parts[2], parts[1], -parts[0]])

def directions(direction_ids):
    ids_float = direction_ids.astype(jnp.float32)
    dir_y = SPREAD * (2.0 * ids_float[:, 0] / (G - 1) - 1.0)
    dir_z = SPREAD * (2.0 * ids_float[:, 1] / (G - 1) - 1.0)
    dir_x = jnp.sqrt(1.0 - dir_y * dir_y - dir_z * dir_z)
    return (dir_x, dir_y, dir_z)

def radiation(dft_block, omegas, plane_x, dir_x, dir_y, dir_z, pos_y):
    cur_real = currents(dft_block[:4])
    cur_imag = currents(dft_block[4:])
    pos_z = jnp.arange(dft_block.shape[3]).astype(jnp.float32)
    phase_z = omegas[:, None, None] * (pos_z[:, None] * dir_z[None, :])[None]
    phase_y = omegas[:, None, None] * (pos_y[:, None] * dir_y[None, :] + plane_x * dir_x[None, :])[None]
    cos_z, sin_z = (jnp.cos(phase_z), jnp.sin(phase_z))
    cos_y, sin_y = (jnp.cos(phase_y), jnp.sin(phase_y))
    part_real = jnp.einsum('cfyz,fzd->cfyd', cur_real, cos_z, precision=BEST_PRECISION) - jnp.einsum('cfyz,fzd->cfyd', cur_imag, sin_z, precision=BEST_PRECISION)
    part_imag = jnp.einsum('cfyz,fzd->cfyd', cur_real, sin_z, precision=BEST_PRECISION) + jnp.einsum('cfyz,fzd->cfyd', cur_imag, cos_z, precision=BEST_PRECISION)
    out_real = lax.optimization_barrier(jnp.sum(part_real * cos_y[None] - part_imag * sin_y[None], axis=2))
    out_imag = lax.optimization_barrier(jnp.sum(part_real * sin_y[None] + part_imag * cos_y[None], axis=2))
    return jnp.concatenate([out_real, out_imag], 0)

def reference(e_field, h_field, polar, polar_rate, material_id, eps_inf, delta_eps, pole_freq, damping, dft_acc, plane_index, direction_ids):
    keep_rate, drive_gain, coupled, e_scale = material_terms(material_id, eps_inf, delta_eps, pole_freq, damping)
    plane_row = plane_index[0]
    samples = []
    for step_index in range(STEPS):
        e_row_rim = jnp.zeros_like(e_field[1:3, :1])
        e_col_rim = jnp.zeros_like(e_field[0:3:2, :, :1])
        h_field = h_field - COURANT * curl_forward(e_field, e_row_rim, e_col_rim)
        rate_new = keep_rate * polar_rate + drive_gain * (coupled * e_field - polar)
        polar = polar + COURANT * rate_new
        h_row_rim = jnp.zeros_like(h_field[1:3, :1])
        h_col_rim = jnp.zeros_like(h_field[0:3:2, :, :1])
        e_field = e_field + e_scale * (curl_backward(h_field, h_row_rim, h_col_rim) - rate_new)
        polar_rate = rate_new
        samples.append(plane_sample(e_field, h_field, plane_row))
    stacked = jnp.stack(samples)
    omegas = frequencies(jnp.arange(F, dtype=jnp.int32), F)
    angles = sample_times(STEPS)[:, None] * omegas[None, :]
    dft_out = update_dft(dft_acc, angles, stacked)
    dir_x, dir_y, dir_z = directions(direction_ids)
    plane_x = plane_row.astype(jnp.float32)
    pos_y = jnp.arange(NY).astype(jnp.float32)
    blocks = jnp.moveaxis(dft_out.reshape(8, F // 8, 8, NY, NZ), 1, 0)
    omega_blocks = omegas.reshape(F // 8, 8)

    def one_block(pair):
        return radiation(pair[0], pair[1], plane_x, dir_x, dir_y, dir_z, pos_y)
    far_blocks = lax.map(one_block, (blocks, omega_blocks))
    far_field = jnp.moveaxis(far_blocks, 0, 1).reshape(8, F, D) * (1.0 / math.sqrt(NY * NZ))
    return (e_field, h_field, polar, polar_rate, dft_out, far_field)
```

```python
import math

import jax
import jax.numpy as jnp
from jax import lax
from jax.experimental import pallas as pl
from jax.experimental.pallas import tpu as pltpu
from jax.sharding import PartitionSpec as P

STEPS = 8
HALO = 8
G = 64
FINE = 16

COURANT = 0.5
OMEGA_LO = 2.0 * math.pi / 24.0
OMEGA_HI = 2.0 * math.pi / 12.0
SPREAD = 0.7

VMEM = pl.BlockSpec(memory_space=pltpu.VMEM)
SMEM = pl.BlockSpec(memory_space=pltpu.SMEM)


def shifted(value, axis, steps):
    count = lax.axis_size(axis)
    first, last = (max(0, -steps), min(count, count - steps))
    return lax.ppermute(value, axis, [(source, source + steps) for source in range(first, last)])


def material_table(eps_inf, delta_eps, pole_freq, damping):
    half_damp = 0.5 * damping
    keep = (1.0 - half_damp) / (1.0 + half_damp)
    drive = pole_freq * pole_freq / COURANT / (1.0 + half_damp)
    return jnp.stack([keep, drive, delta_eps, COURANT / eps_inf])


def yee_kernel(
    where_ref, table_ref, own_ref, ylo_ref, yhi_ref, xlo_ref, xhi_ref, clo_ref, chi_ref,
    e_out, h_out, p_out, j_out, sample_out, state, coef,
):
    cells_x, cells_y, cells_z = own_ref.shape[1:]
    wide_x = cells_x + 2 * HALO
    wide_y = cells_y + 2 * HALO
    inner_x, inner_y = (HALO, HALO + cells_x), (HALO, HALO + cells_y)
    x_spans = ((0, HALO), inner_x, (inner_x[1], wide_x))
    y_spans = ((0, HALO), inner_y, (inner_y[1], wide_y))
    parts = (
        ((clo_ref, 0), (xlo_ref, None), (clo_ref, 1)),
        ((ylo_ref, None), (own_ref, None), (yhi_ref, None)),
        ((chi_ref, 0), (xhi_ref, None), (chi_ref, 1)),
    )
    levels = table_ref.shape[1]
    for i, (x0, x1) in enumerate(x_spans):
        for k, (y0, y1) in enumerate(y_spans):
            ref, lead = parts[i][k]
            part = ref if lead is None else ref.at[lead]
            inside = jnp.float32(1.0)
            if i != 1:
                inside = inside * where_ref[0, i // 2]
            if k != 1:
                inside = inside * where_ref[1, k // 2]

            def fill(x, carry, part=part, inside=inside, x0=x0, y0=y0, y1=y1):
                for comp in range(12):
                    state[comp, x0 + x, y0:y1, :] = part[comp, x]
                ids = part[12, x]
                values = [jnp.zeros_like(ids)] * 4
                for level in range(levels):
                    hit = ids == jnp.float32(level)
                    values = [jnp.where(hit, table_ref[c, level], v) for c, v in enumerate(values)]
                coef[0, x0 + x, y0:y1, :] = values[0]
                coef[1, x0 + x, y0:y1, :] = values[1]
                coef[2, x0 + x, y0:y1, :] = values[2]
                coef[3, x0 + x, y0:y1, :] = values[3] * inside
                coef[4, x0 + x, y0:y1, :] = jnp.full_like(ids, COURANT) * inside
                return carry

            lax.fori_loop(0, x1 - x0, fill, 0)

    lane = lax.broadcasted_iota(jnp.int32, (wide_y, cells_z), 1)
    not_last = lane < cells_z - 1
    not_first = lane > 0

    def z_next(v):
        return jnp.where(not_last, pltpu.roll(v, cells_z - 1, 1), 0.0)

    def z_prev(v):
        return jnp.where(not_first, pltpu.roll(v, 1, 1), 0.0)

    def y_next(v):
        return pltpu.roll(v, wide_y - 1, 0)

    def y_prev(v):
        return pltpu.roll(v, 1, 0)

    def magnetic(x):
        ex, ey, ez = (state[c, x] for c in range(3))
        ey_x, ez_x = (state[1, x + 1], state[2, x + 1])
        gain = coef[4, x]
        hx = state[3, x] - gain * ((y_next(ez) - ez) - (z_next(ey) - ey))
        hy = state[4, x] - gain * ((z_next(ex) - ex) - (ez_x - ez))
        hz = state[5, x] - gain * ((ey_x - ey) - (y_next(ex) - ex))
        state[3, x] = hx
        state[4, x] = hy
        state[5, x] = hz
        return hx, hy, hz

    def both(x, carry):
        hy_x, hz_x = (state[4, x - 1], state[5, x - 1])
        fields = [state[c, x] for c in range(3)]
        hx, hy, hz = magnetic(x)
        curl = (
            (hz - y_prev(hz)) - (hy - z_prev(hy)),
            (hx - z_prev(hx)) - (hz - hz_x),
            (hy - hy_x) - (hx - y_prev(hx)),
        )
        keep, drive, coupled, scale = (coef[c, x] for c in range(4))
        for c in range(3):
            polar = state[6 + c, x]
            rate = keep * state[9 + c, x] + drive * (coupled * fields[c] - polar)
            state[6 + c, x] = polar + COURANT * rate
            state[9 + c, x] = rate
            state[c, x] = fields[c] + scale * (curl[c] - rate)
        return carry

    plane = HALO + where_ref_row(where_ref)
    for step in range(STEPS):
        magnetic(step)
        lax.fori_loop(step + 1, wide_x - 1 - step, both, 0, unroll=2)
        for slot, comp in enumerate((1, 2, 4, 5)):
            sample_out[step, slot] = state[comp, plane, inner_y[0] : inner_y[1], :]
    for c in range(3):
        for base, out in ((0, e_out), (3, h_out), (6, p_out), (9, j_out)):
            out[c] = state[base + c, inner_x[0] : inner_x[1], inner_y[0] : inner_y[1], :]


def where_ref_row(where_ref):
    return where_ref[2, 0].astype(jnp.int32)


def yee_steps(where, table, own, ylo, yhi, xlo, xhi, clo, chi):
    cells = own.shape[1:]
    block = jax.ShapeDtypeStruct((3,) + cells, jnp.float32)
    wide = (cells[0] + 2 * HALO, cells[1] + 2 * HALO, cells[2])
    return pl.pallas_call(
        yee_kernel,
        out_shape=[block] * 4 + [jax.ShapeDtypeStruct((STEPS, 4) + cells[1:], jnp.float32)],
        in_specs=[SMEM, SMEM] + [VMEM] * 7,
        out_specs=[VMEM] * 5,
        scratch_shapes=[
            pltpu.VMEM((12,) + wide, jnp.float32),
            pltpu.VMEM((5,) + wide, jnp.float32),
        ],
        compiler_params=pltpu.CompilerParams(vmem_limit_bytes=40 * 1024 * 1024),
        name="yee_steps",
    )(where, table, own, ylo, yhi, xlo, xhi, clo, chi)


def halves(value):
    high = value.astype(jnp.bfloat16)
    return high, (value - high.astype(jnp.float32)).astype(jnp.bfloat16)


def phase_kernel(coarse_c, coarse_s, fine_c, fine_s, high_out, low_out):
    freqs, coarse, count = coarse_c.shape

    def one(f, carry):
        fc, fs = fine_c[f], fine_s[f]
        for a in range(coarse):
            cc, cs = coarse_c[f, a : a + 1], coarse_s[f, a : a + 1]
            rows = slice(a * FINE, (a + 1) * FINE)
            cos_high, cos_low = halves(cc * fc - cs * fs)
            sin_high, sin_low = halves(cs * fc + cc * fs)
            high_out[f, rows, :count] = cos_high
            high_out[f, rows, count:] = sin_high
            low_out[f, rows, :count] = cos_low
            low_out[f, rows, count:] = sin_low
        return carry

    lax.fori_loop(0, freqs, one, 0)


def z_phases(omegas, dir_z, cells_z):
    coarse = cells_z // FINE
    base = omegas[:, None, None] * (
        (FINE * jnp.arange(coarse)).astype(jnp.float32)[:, None] * dir_z[None, :]
    )
    fine = omegas[:, None, None] * (jnp.arange(FINE).astype(jnp.float32)[:, None] * dir_z[None, :])
    out = jax.ShapeDtypeStruct(
        (omegas.shape[0], cells_z, 2 * dir_z.shape[0]), jnp.bfloat16
    )
    return pl.pallas_call(
        phase_kernel,
        out_shape=[out, out],
        in_specs=[VMEM] * 4,
        out_specs=[VMEM] * 2,
        cost_estimate=pl.CostEstimate(flops=8000000, bytes_accessed=3000000, transcendentals=0),
        name="z_phases",
    )(jnp.cos(base), jnp.sin(base), jnp.cos(fine), jnp.sin(fine))


def radiation_kernel(
    cos_ref, sin_ref, sample_ref, acc_ref, high_ref, low_ref, cosy_ref, siny_ref,
    dft_out, part_out, rows_ref,
):
    freqs, cells_y, cells_z = acc_ref.shape[1:]
    steps = sample_ref.shape[0]
    count = cosy_ref.shape[2]
    half = 4 * cells_y

    def one(f, carry):
        reals, imags = [], []
        for c in range(4):
            real = acc_ref[c, f]
            imag = acc_ref[4 + c, f]
            for n in range(steps):
                sample = sample_ref[n, c]
                real = real + cos_ref[n, f] * sample
                imag = imag - sin_ref[n, f] * sample
            dft_out[c, f] = real
            dft_out[4 + c, f] = imag
            reals.append(real)
            imags.append(imag)
        left_high, left_low = halves(jnp.concatenate(reals + imags, axis=0))
        high, low = high_ref[f], low_ref[f]

        def mul(a, b):
            return jnp.dot(a, b, preferred_element_type=jnp.float32)

        table = mul(left_high, high) + (mul(left_high, low) + mul(left_low, high))
        part_real = table[:half, :count] - table[half:, count:]
        part_imag = table[:half, count:] + table[half:, :count]
        cos_y, sin_y = cosy_ref[f], siny_ref[f]
        for c, (source, sign) in enumerate(((3, -1.0), (2, 1.0), (1, 1.0), (0, -1.0))):
            pr = part_real[source * cells_y : (source + 1) * cells_y]
            pi = part_imag[source * cells_y : (source + 1) * cells_y]
            out_real = jnp.sum(pr * cos_y - pi * sin_y, axis=0, keepdims=True)
            out_imag = jnp.sum(pr * sin_y + pi * cos_y, axis=0, keepdims=True)
            rows_ref[c, pl.ds(f, 1), :] = sign * out_real
            rows_ref[4 + c, pl.ds(f, 1), :] = sign * out_imag
        return carry

    lax.fori_loop(0, freqs, one, 0)
    rows = jnp.concatenate([rows_ref[c] for c in range(8)] * 2, axis=0)
    part_out[...] = rows.T


def radiate(cos_a, sin_a, samples, acc, high, low, cos_y, sin_y):
    count = cos_y.shape[2]
    freqs = acc.shape[1]
    return pl.pallas_call(
        radiation_kernel,
        out_shape=[
            jax.ShapeDtypeStruct(acc.shape, jnp.float32),
            jax.ShapeDtypeStruct((count, 16 * freqs), jnp.float32),
        ],
        in_specs=[SMEM, SMEM] + [VMEM] * 6,
        out_specs=[VMEM] * 2,
        scratch_shapes=[pltpu.VMEM((8, freqs, count), jnp.float32)],
        compiler_params=pltpu.CompilerParams(vmem_limit_bytes=40 * 1024 * 1024),
        name="radiate",
    )(cos_a, sin_a, samples, acc, high, low, cos_y, sin_y)


def spread_rows(samples, root):
    count = lax.axis_size("rows")
    pieces = samples.reshape(count, -1, samples.shape[-1])
    arrived = lax.all_to_all(pieces, "rows", split_axis=0, concat_axis=0, tiled=True)
    mine = lax.dynamic_index_in_dim(arrived, root, 0, keepdims=True)
    copies = jnp.broadcast_to(mine, pieces.shape)
    gathered = lax.all_to_all(copies, "rows", split_axis=0, concat_axis=0, tiled=True)
    return gathered.reshape(samples.shape)


def local(
    e_field, h_field, polar, polar_rate, material_id, eps_inf, delta_eps, pole_freq, damping,
    dft_acc, plane_index, direction_ids,
):
    cells_x, cells_y, cells_z = e_field.shape[1:]
    freq_block = dft_acc.shape[1]
    row, col = lax.axis_index("rows"), lax.axis_index("cols")
    rows, cols = lax.axis_size("rows"), lax.axis_size("cols")

    mats = material_id.astype(jnp.float32)[None]
    fields = (e_field, h_field, polar, polar_rate, mats)
    own = jnp.concatenate(fields, 0)
    first = jnp.concatenate([v[:, :, :HALO] for v in fields], 0)
    final = jnp.concatenate([v[:, :, -HALO:] for v in fields], 0)
    yhi = shifted(first, "cols", -1)
    ylo = shifted(final, "cols", 1)
    xhi = shifted(own, "rows", -1)
    xlo = shifted(own, "rows", 1)
    sides = jnp.stack([ylo, yhi])
    chi = shifted(sides, "rows", -1)
    clo = shifted(sides, "rows", 1)

    plane_row = plane_index[0]
    root_row = plane_row // cells_x
    local_row = plane_row % cells_x
    table = material_table(eps_inf, delta_eps, pole_freq, damping)
    where = jnp.stack(
        [row > 0, row < rows - 1, col > 0, col < cols - 1, local_row, local_row]
    ).astype(jnp.float32).reshape(3, 2)
    e_out, h_out, p_out, j_out, samples = yee_steps(
        where, table, own, ylo, yhi, xlo, xhi, clo, chi
    )

    total_f = rows * freq_block
    freq_ids = row * freq_block + jnp.arange(freq_block, dtype=jnp.int32)
    omegas = OMEGA_LO + (OMEGA_HI - OMEGA_LO) * (freq_ids.astype(jnp.float32) / (total_f - 1))
    times = (jnp.arange(STEPS).astype(jnp.float32) + 1.0) * COURANT
    angles = times[:, None] * omegas[None, :]
    ids_float = direction_ids.astype(jnp.float32)
    dir_y = SPREAD * (2.0 * ids_float[:, 0] / (G - 1) - 1.0)
    dir_z = SPREAD * (2.0 * ids_float[:, 1] / (G - 1) - 1.0)
    dir_x = jnp.sqrt(1.0 - dir_y * dir_y - dir_z * dir_z)
    pos_y = (col * cells_y + jnp.arange(cells_y, dtype=jnp.int32)).astype(jnp.float32)
    plane_x = plane_row.astype(jnp.float32)
    phase_y = (
        omegas[:, None, None] * (pos_y[:, None] * dir_y[None, :] + plane_x * dir_x[None, :])[None]
    )
    high, low = z_phases(omegas, dir_z, cells_z)

    received = spread_rows(samples, root_row)
    dft_out, partial_sum = radiate(
        jnp.cos(angles), jnp.sin(angles), received, dft_acc, high, low,
        jnp.cos(phase_y), jnp.sin(phase_y),
    )
    pieces = partial_sum.reshape(cols, -1, partial_sum.shape[-1])
    arrived = lax.all_to_all(pieces, "cols", split_axis=0, concat_axis=0, tiled=True)
    scale = 1.0 / math.sqrt(cols * cells_y * cells_z)
    far = jnp.sum(arrived, axis=0) * scale
    far_field = far[:, : 8 * freq_block].T.reshape(8, freq_block, -1)
    return (e_out, h_out, p_out, j_out, dft_out, far_field)


def solution(mesh):
    grid = P(None, "rows", "cols", None)
    in_specs = (
        grid, grid, grid, grid, P("rows", "cols", None), P(), P(), P(), P(), grid, P(), P(),
    )
    out_specs = (grid, grid, grid, grid, grid, P(None, "rows", "cols"))
    return jax.shard_map(local, mesh=mesh, in_specs=in_specs, out_specs=out_specs, check_vma=False)
```

```python
import math

import jax
import jax.numpy as jnp
from jax import lax
from jax.experimental import pallas as pl
from jax.experimental.pallas import tpu as pltpu
from jax.sharding import PartitionSpec as P


STEPS = 8
HALO = 8
G = 64
FINE = 16

COURANT = 0.5
OMEGA_LO = 2.0 * math.pi / 24.0
OMEGA_HI = 2.0 * math.pi / 12.0
SPREAD = 0.7

VMEM = pl.BlockSpec(memory_space=pltpu.VMEM)
SMEM = pl.BlockSpec(memory_space=pltpu.SMEM)


def shifted(value, axis, steps):
    count = lax.axis_size(axis)
    first, last = (max(0, -steps), min(count, count - steps))
    return lax.ppermute(value, axis, [(source, source + steps) for source in range(first, last)])


def material_table(eps_inf, delta_eps, pole_freq, damping):
    half_damp = 0.5 * damping
    keep = (1.0 - half_damp) / (1.0 + half_damp)
    drive = pole_freq * pole_freq / COURANT / (1.0 + half_damp)
    table = jnp.stack([keep, 0.5 * drive, 4.0 * delta_eps, 0.5 * (COURANT / eps_inf)])
    return jnp.broadcast_to(
        jnp.pad(table, ((0, 0), (0, 128 - table.shape[1])))[:, None, :], (4, 8, 128)
    )


def pack_kernel(e_ref, h_ref, p_ref, j_ref, m_ref, own, first, final, mats, sems):
    cells_y = e_ref.shape[2]
    spans = ((own, 0, cells_y), (first, 0, HALO), (final, cells_y - HALO, HALO))
    copies = [pltpu.make_async_copy(m_ref, mats, sems.at[0])]
    for i, ref in enumerate((e_ref, h_ref, p_ref, j_ref)):
        for k, (out, start, size) in enumerate(spans):
            copies.append(
                pltpu.make_async_copy(
                    ref.at[:, :, pl.ds(start, size), :],
                    out.at[pl.ds(3 * i, 3)],
                    sems.at[1 + 3 * i + k],
                )
            )
    for copy in copies:
        copy.start()
    copies[0].wait()
    ids = mats[...].astype(jnp.float32)
    own[12] = ids
    first[12] = ids[:, :HALO]
    final[12] = ids[:, cells_y - HALO :]
    for copy in copies[1:]:
        copy.wait()


def pack(e_field, h_field, polar, polar_rate, material_id):
    cells_x, cells_y, cells_z = material_id.shape
    strip = jax.ShapeDtypeStruct((13, cells_x, HALO, cells_z), jnp.float32)
    return pl.pallas_call(
        pack_kernel,
        out_shape=[
            jax.ShapeDtypeStruct((13, cells_x, cells_y, cells_z), jnp.float32), strip, strip,
        ],
        in_specs=[pl.BlockSpec(memory_space=pltpu.HBM)] * 5,
        out_specs=[VMEM] * 3,
        scratch_shapes=[
            pltpu.VMEM(material_id.shape, jnp.int32),
            pltpu.SemaphoreType.DMA((13,)),
        ],
        compiler_params=pltpu.CompilerParams(vmem_limit_bytes=8 * 1024 * 1024),
        name="pack",
    )(
        *(
            pltpu.with_memory_space_constraint(v, pltpu.HBM)
            for v in (e_field, h_field, polar, polar_rate, material_id)
        )
    )


def yee_kernel(
    where_ref, table_ref, own_ref, ylo_ref, yhi_ref, xlo_ref, xhi_ref, clo_ref, chi_ref,
    e_out, h_out, p_out, j_out, sample_out, even, odd, coef,
):
    cells_x, cells_y, cells_z = own_ref.shape[1:]
    wide_x = cells_x + 2 * HALO
    wide_y = cells_y + 2 * HALO
    inner_x, inner_y = (HALO, HALO + cells_x), (HALO, HALO + cells_y)
    x_spans = ((0, HALO), inner_x, (inner_x[1], wide_x))
    y_spans = ((0, HALO), inner_y, (inner_y[1], wide_y))
    parts = (
        ((clo_ref, 0), (xlo_ref, None), (clo_ref, 1)),
        ((ylo_ref, None), (own_ref, None), (yhi_ref, None)),
        ((chi_ref, 0), (xhi_ref, None), (chi_ref, 1)),
    )
    gains = (1.0, 2.0, 4.0, 2.0)
    whole = slice(0, wide_y)
    zeros = jnp.zeros((HALO, cells_z), jnp.float32)
    tables = [table_ref[c] for c in range(4)]
    for i, (x0, x1) in enumerate(x_spans):
        for k, (y0, y1) in enumerate(y_spans):
            ref, lead = parts[i][k]
            part = ref if lead is None else ref.at[lead]
            inside = jnp.float32(1.0)
            if i != 1:
                inside = inside * where_ref[0, i // 2].astype(jnp.float32)
            if k != 1:
                inside = inside * where_ref[1, k // 2].astype(jnp.float32)

            def fill(x, carry, part=part, inside=inside, x0=x0, y0=y0, y1=y1):
                for comp in range(12):
                    even[comp, x0 + x, y0:y1, :] = part[comp, x] * gains[comp // 3]
                for y in range(y0, y1, 8):
                    ids = part[12, x, y - y0 : y - y0 + 8, :].astype(jnp.int32)
                    for c in range(4):
                        value = jnp.take_along_axis(tables[c], ids, axis=1)
                        coef[c, x0 + x, y : y + 8, :] = value * inside if c == 3 else value
                return carry

            lax.fori_loop(0, x1 - x0, fill, 0, unroll=2)
    for buffer in (even, odd):
        for comp in (0, 2):
            for x in range(wide_x):
                buffer[comp, x, wide_y:, :] = zeros

    lane = lax.broadcasted_iota(jnp.int32, (wide_y, cells_z), 1)
    not_last = lane < cells_z - 1
    not_first = lane > 0
    x_edge = where_ref[0, 0].astype(jnp.float32)
    y_edge = where_ref[1, 0].astype(jnp.float32)
    plane = HALO + where_ref[2, 0]

    def z_next(v):
        return jnp.where(not_last, pltpu.roll(v, cells_z - 1, 1), 0.0)

    def z_prev(v):
        return jnp.where(not_first, pltpu.roll(v, 1, 1), 0.0)

    def y_prev(v):
        return pltpu.roll(jnp.concatenate([v[:HALO] * y_edge, v[HALO:]], axis=0), 1, 0)

    for step in range(STEPS):
        old, new = (even, odd) if step % 2 == 0 else (odd, even)

        def magnetic(x, old=old):
            ex, ey, ez = (old[c, x, whole] for c in range(3))
            ey_x, ez_x = (old[1, x + 1, whole], old[2, x + 1, whole])
            ex_y, ez_y = (old[0, x, 1 : wide_y + 1], old[2, x, 1 : wide_y + 1])
            hx = old[3, x, whole] - ((ez_y - ez) - (z_next(ey) - ey))
            hy = old[4, x, whole] - ((z_next(ex) - ex) - (ez_x - ez))
            hz = old[5, x, whole] - ((ey_x - ey) - (ex_y - ex))
            return hx, hy, hz

        def electric(x, old=old, new=new):
            edge = jnp.where(x == HALO, x_edge, 1.0)
            hx, hy, hz = (new[3 + c, x, whole] for c in range(3))
            hy_x, hz_x = (new[c, x - 1, whole] * edge for c in (4, 5))
            curl = (
                (hz - y_prev(hz)) - (hy - z_prev(hy)),
                (hx - z_prev(hx)) - (hz - hz_x),
                (hy - hy_x) - (hx - y_prev(hx)),
            )
            keep, drive, coupled, scale = (coef[c, x] for c in range(4))
            for c in range(3):
                polar = old[6 + c, x, whole]
                field = old[c, x, whole]
                rate = keep * old[9 + c, x, whole] + drive * (coupled * field - polar)
                new[6 + c, x, whole] = polar + rate
                new[9 + c, x, whole] = rate
                new[c, x, whole] = field + scale * (curl[c] - rate)

        def put(x, values, new=new):
            for c in range(3):
                new[3 + c, x, whole] = values[c]

        def both(x, carry, magnetic=magnetic, electric=electric, put=put):
            after = magnetic(x + 1)
            electric(x)
            put(x + 1, after)
            return carry

        put(step, magnetic(step))
        put(step + 1, magnetic(step + 1))
        lax.fori_loop(step + 1, wide_x - 2 - step, both, 0)
        electric(wide_x - 2 - step)
        for slot, (comp, gain) in enumerate(((1, 1.0), (2, 1.0), (4, 0.5), (5, 0.5))):
            sample_out[step, slot] = new[comp, plane, inner_y[0] : inner_y[1], :] * gain

    final = even if STEPS % 2 == 0 else odd

    def emit(x, carry):
        for c in range(3):
            for base, out, gain in ((0, e_out, 1.0), (3, h_out, 0.5), (6, p_out, 0.25), (9, j_out, 0.5)):
                out[c, x] = final[base + c, HALO + x, inner_y[0] : inner_y[1], :] * gain
        return carry

    lax.fori_loop(0, cells_x, emit, 0, unroll=2)


def yee_steps(where, table, own, ylo, yhi, xlo, xhi, clo, chi):
    cells = own.shape[1:]
    block = jax.ShapeDtypeStruct((3,) + cells, jnp.float32)
    wide = (cells[0] + 2 * HALO, cells[1] + 2 * HALO, cells[2])
    state = pltpu.VMEM((12, wide[0], wide[1] + 8, wide[2]), jnp.float32)
    return pl.pallas_call(
        yee_kernel,
        out_shape=[block] * 4 + [jax.ShapeDtypeStruct((STEPS, 4) + cells[1:], jnp.float32)],
        in_specs=[SMEM, VMEM] + [VMEM] * 7,
        out_specs=[VMEM] * 5,
        scratch_shapes=[state, state, pltpu.VMEM((4,) + wide, jnp.float32)],
        compiler_params=pltpu.CompilerParams(vmem_limit_bytes=20 * 1024 * 1024),
        name="yee_steps",
    )(where, table, own, ylo, yhi, xlo, xhi, clo, chi)


def halves(value):
    high = value.astype(jnp.bfloat16)
    return high, (value - high.astype(jnp.float32)).astype(jnp.bfloat16)


def phase_kernel(coarse_c, coarse_s, fine_c, fine_s, high_out, low_out):
    freqs, coarse, count = coarse_c.shape

    def one(f, carry):
        fc, fs = fine_c[f], fine_s[f]
        for a in range(coarse):
            cc, cs = coarse_c[f, a : a + 1], coarse_s[f, a : a + 1]
            rows = slice(a * FINE, (a + 1) * FINE)
            cos_high, cos_low = halves(cc * fc - cs * fs)
            sin_high, sin_low = halves(cs * fc + cc * fs)
            high_out[f, rows, :count] = cos_high
            high_out[f, rows, count:] = sin_high
            low_out[f, rows, :count] = cos_low
            low_out[f, rows, count:] = sin_low
        return carry

    lax.fori_loop(0, freqs, one, 0)


def z_phases(omegas, dir_z, cells_z):
    coarse = cells_z // FINE
    base = omegas[:, None, None] * (
        (FINE * jnp.arange(coarse)).astype(jnp.float32)[:, None] * dir_z[None, :]
    )
    fine = omegas[:, None, None] * (jnp.arange(FINE).astype(jnp.float32)[:, None] * dir_z[None, :])
    out = jax.ShapeDtypeStruct(
        (omegas.shape[0], cells_z, 2 * dir_z.shape[0]), jnp.bfloat16
    )
    return pl.pallas_call(
        phase_kernel,
        out_shape=[out, out],
        in_specs=[VMEM] * 4,
        out_specs=[VMEM] * 2,
        compiler_params=pltpu.CompilerParams(vmem_limit_bytes=8 * 1024 * 1024),
        cost_estimate=pl.CostEstimate(flops=8000000, bytes_accessed=3000000, transcendentals=0),
        name="z_phases",
    )(jnp.cos(base), jnp.sin(base), jnp.cos(fine), jnp.sin(fine))


def radiation_kernel(
    cos_ref, sin_ref, sample_ref, acc_ref, high_ref, low_ref, cosy_ref, siny_ref,
    dft_out, part_out, rows_ref,
):
    freqs, cells_y, _ = acc_ref.shape[1:]
    steps = sample_ref.shape[0]
    count = cosy_ref.shape[2]
    half = 4 * cells_y

    def one(f, carry):
        reals, imags = [], []
        for c in range(4):
            real = acc_ref[c, f]
            imag = acc_ref[4 + c, f]
            for n in range(steps):
                sample = sample_ref[n, c]
                real = real + cos_ref[n, f] * sample
                imag = imag - sin_ref[n, f] * sample
            dft_out[c, f] = real
            dft_out[4 + c, f] = imag
            reals.append(real)
            imags.append(imag)
        left_high, left_low = halves(jnp.concatenate(reals + imags, axis=0))
        high, low = high_ref[f], low_ref[f]

        def mul(a, b):
            return jnp.dot(a, b, preferred_element_type=jnp.float32)

        table = mul(left_high, high) + (mul(left_high, low) + mul(left_low, high))
        part_real = table[:half, :count] - table[half:, count:]
        part_imag = table[:half, count:] + table[half:, :count]
        cos_y, sin_y = cosy_ref[f], siny_ref[f]
        for c, (source, sign) in enumerate(((3, -1.0), (2, 1.0), (1, 1.0), (0, -1.0))):
            pr = part_real[source * cells_y : (source + 1) * cells_y]
            pi = part_imag[source * cells_y : (source + 1) * cells_y]
            out_real = jnp.sum(pr * cos_y - pi * sin_y, axis=0, keepdims=True)
            out_imag = jnp.sum(pr * sin_y + pi * cos_y, axis=0, keepdims=True)
            rows_ref[c, pl.ds(f, 1), :] = sign * out_real
            rows_ref[4 + c, pl.ds(f, 1), :] = sign * out_imag
        return carry

    lax.fori_loop(0, freqs, one, 0)
    half_count = count // 2
    rows = jnp.concatenate(
        [rows_ref[c, :, k * half_count : (k + 1) * half_count] for k in range(2) for c in range(8)],
        axis=0,
    )
    part_out[...] = rows.T


def radiate(cos_a, sin_a, samples, acc, high, low, cos_y, sin_y):
    count = cos_y.shape[2]
    freqs = acc.shape[1]
    return pl.pallas_call(
        radiation_kernel,
        out_shape=[
            jax.ShapeDtypeStruct(acc.shape, jnp.float32),
            jax.ShapeDtypeStruct((count // 2, 16 * freqs), jnp.float32),
        ],
        in_specs=[SMEM, SMEM] + [VMEM] * 6,
        out_specs=[VMEM] * 2,
        scratch_shapes=[pltpu.VMEM((8, freqs, count), jnp.float32)],
        compiler_params=pltpu.CompilerParams(vmem_limit_bytes=16 * 1024 * 1024),
        name="radiate",
    )(cos_a, sin_a, samples, acc, high, low, cos_y, sin_y)


def finish(arrived, scale, freqs):
    share = 2 * arrived.shape[1]

    def finish_kernel(in_ref, out_ref):
        total = jnp.sum(in_ref[...], axis=0) * scale
        half = total.shape[1] // 2
        both = jnp.concatenate([total, pltpu.roll(total, half, 1)], axis=0)
        out_ref[...] = both.T[:half].reshape(out_ref.shape)

    return pl.pallas_call(
        finish_kernel,
        out_shape=jax.ShapeDtypeStruct((8, freqs, share), jnp.float32),
        in_specs=[VMEM],
        out_specs=VMEM,
        compiler_params=pltpu.CompilerParams(vmem_limit_bytes=4 * 1024 * 1024),
        name="finish",
    )(arrived)


def spread_rows(samples, root):
    count = lax.axis_size("rows")
    pieces = samples.reshape(count, -1, samples.shape[-1])
    arrived = lax.all_to_all(pieces, "rows", split_axis=0, concat_axis=0, tiled=True)
    mine = lax.dynamic_index_in_dim(arrived, root, 0, keepdims=True)
    copies = jnp.broadcast_to(mine, pieces.shape)
    gathered = lax.all_to_all(copies, "rows", split_axis=0, concat_axis=0, tiled=True)
    return gathered.reshape(samples.shape)


def local(
    e_field, h_field, polar, polar_rate, material_id, eps_inf, delta_eps, pole_freq, damping,
    dft_acc, plane_index, direction_ids,
):
    cells_x, cells_y, cells_z = e_field.shape[1:]
    freq_block = dft_acc.shape[1]
    row, col = lax.axis_index("rows"), lax.axis_index("cols")
    rows, cols = lax.axis_size("rows"), lax.axis_size("cols")

    own, first, final = pack(e_field, h_field, polar, polar_rate, material_id)
    yhi = shifted(first, "cols", -1)
    ylo = shifted(final, "cols", 1)
    xhi = shifted(own, "rows", -1)
    xlo = shifted(own, "rows", 1)
    sides = jnp.stack([ylo, yhi])
    chi = shifted(sides, "rows", -1)
    clo = shifted(sides, "rows", 1)

    plane_row = plane_index[0]
    root_row = plane_row // cells_x
    local_row = plane_row % cells_x
    table = material_table(eps_inf, delta_eps, pole_freq, damping)
    where = jnp.stack(
        [row > 0, row < rows - 1, col > 0, col < cols - 1, local_row, local_row]
    ).astype(jnp.int32).reshape(3, 2)

    total_f = rows * freq_block
    freq_ids = row * freq_block + jnp.arange(freq_block, dtype=jnp.int32)
    omegas = OMEGA_LO + (OMEGA_HI - OMEGA_LO) * (freq_ids.astype(jnp.float32) / (total_f - 1))
    times = (jnp.arange(STEPS).astype(jnp.float32) + 1.0) * COURANT
    angles = times[:, None] * omegas[None, :]
    count = direction_ids.shape[0]
    share = count // cols
    pairs = direction_ids.reshape(cols, 2, share // 2, 2).transpose(1, 0, 2, 3)
    ids_float = pairs.reshape(count, 2).astype(jnp.float32)
    dir_y = SPREAD * (2.0 * ids_float[:, 0] / (G - 1) - 1.0)
    dir_z = SPREAD * (2.0 * ids_float[:, 1] / (G - 1) - 1.0)
    dir_x = jnp.sqrt(1.0 - dir_y * dir_y - dir_z * dir_z)
    pos_y = (col * cells_y + jnp.arange(cells_y, dtype=jnp.int32)).astype(jnp.float32)
    plane_x = plane_row.astype(jnp.float32)
    phase_y = (
        omegas[:, None, None] * (pos_y[:, None] * dir_y[None, :] + plane_x * dir_x[None, :])[None]
    )
    high, low = z_phases(omegas, dir_z, cells_z)
    waves = (
        high, low, jnp.cos(phase_y), jnp.sin(phase_y), jnp.cos(angles), jnp.sin(angles), where, table,
    )
    waves, (xlo, xhi, clo, chi) = lax.optimization_barrier((waves, (xlo, xhi, clo, chi)))
    high, low, cos_y, sin_y, cos_a, sin_a, where, table = waves
    e_out, h_out, p_out, j_out, samples = yee_steps(
        where, table, own, ylo, yhi, xlo, xhi, clo, chi
    )
    received = spread_rows(samples, root_row)
    dft_out, partial_sum = radiate(
        cos_a, sin_a, received, dft_acc, high, low, cos_y, sin_y,
    )
    pieces = partial_sum.reshape(cols, -1, partial_sum.shape[-1])
    arrived = lax.all_to_all(pieces, "cols", split_axis=0, concat_axis=0, tiled=True)
    far_field = finish(arrived, 1.0 / math.sqrt(cols * cells_y * cells_z), freq_block)
    return (e_out, h_out, p_out, j_out, dft_out, far_field)


def solution(mesh):
    grid = P(None, "rows", "cols", None)
    in_specs = (
        grid, grid, grid, grid, P("rows", "cols", None), P(), P(), P(), P(), grid, P(), P(),
    )
    out_specs = (grid, grid, grid, grid, grid, P(None, "rows", "cols"))
    return jax.shard_map(local, mesh=mesh, in_specs=in_specs, out_specs=out_specs, check_vma=False)
```

```python
import math

import jax
import jax.numpy as jnp
from jax import lax
from jax.experimental import pallas as pl
from jax.experimental.pallas import tpu as pltpu
from jax.sharding import PartitionSpec as P


STEPS = 8
HALO = 8
G = 64
FINE = 16

COURANT = 0.5
OMEGA_LO = 2.0 * math.pi / 24.0
OMEGA_HI = 2.0 * math.pi / 12.0
SPREAD = 0.7

VMEM = pl.BlockSpec(memory_space=pltpu.VMEM)
SMEM = pl.BlockSpec(memory_space=pltpu.SMEM)


def shifted(value, axis, steps):
    count = lax.axis_size(axis)
    first, last = (max(0, -steps), min(count, count - steps))
    return lax.ppermute(value, axis, [(source, source + steps) for source in range(first, last)])


def material_table(eps_inf, delta_eps, pole_freq, damping):
    half_damp = 0.5 * damping
    keep = (1.0 - half_damp) / (1.0 + half_damp)
    drive = pole_freq * pole_freq / COURANT / (1.0 + half_damp)
    table = jnp.stack([keep, 0.5 * drive, 4.0 * delta_eps, 0.5 * (COURANT / eps_inf)])
    return jnp.broadcast_to(
        jnp.pad(table, ((0, 0), (0, 128 - table.shape[1])))[:, None, :], (4, 8, 128)
    )


def pack_kernel(e_ref, h_ref, p_ref, j_ref, m_ref, own, first, final, mats, sems):
    cells_y = e_ref.shape[2]
    spans = ((own, 0, cells_y), (first, 0, HALO), (final, cells_y - HALO, HALO))
    copies = [pltpu.make_async_copy(m_ref, mats, sems.at[0])]
    for i, ref in enumerate((e_ref, h_ref, p_ref, j_ref)):
        for k, (out, start, size) in enumerate(spans):
            copies.append(
                pltpu.make_async_copy(
                    ref.at[:, :, pl.ds(start, size), :],
                    out.at[pl.ds(3 * i, 3)],
                    sems.at[1 + 3 * i + k],
                )
            )
    for copy in copies:
        copy.start()
    copies[0].wait()
    ids = mats[...].astype(jnp.float32)
    own[12] = ids
    first[12] = ids[:, :HALO]
    final[12] = ids[:, cells_y - HALO :]
    for copy in copies[1:]:
        copy.wait()


def pack(e_field, h_field, polar, polar_rate, material_id):
    cells_x, cells_y, cells_z = material_id.shape
    strip = jax.ShapeDtypeStruct((13, cells_x, HALO, cells_z), jnp.float32)
    return pl.pallas_call(
        pack_kernel,
        out_shape=[
            jax.ShapeDtypeStruct((13, cells_x, cells_y, cells_z), jnp.float32), strip, strip,
        ],
        in_specs=[pl.BlockSpec(memory_space=pltpu.HBM)] * 5,
        out_specs=[VMEM] * 3,
        scratch_shapes=[
            pltpu.VMEM(material_id.shape, jnp.int32),
            pltpu.SemaphoreType.DMA((13,)),
        ],
        compiler_params=pltpu.CompilerParams(vmem_limit_bytes=8 * 1024 * 1024),
        name="pack",
    )(
        *(
            pltpu.with_memory_space_constraint(v, pltpu.HBM)
            for v in (e_field, h_field, polar, polar_rate, material_id)
        )
    )


def yee_kernel(
    where_ref, table_ref, own_ref, ylo_ref, yhi_ref, xlo_ref, xhi_ref, ll_ref, lh_ref, hl_ref, hh_ref,
    e_out, h_out, p_out, j_out, sample_out, even, odd, coef,
):
    cells_x, cells_y, cells_z = own_ref.shape[1:]
    wide_x = cells_x + 2 * HALO
    wide_y = cells_y + 2 * HALO
    inner_x, inner_y = (HALO, HALO + cells_x), (HALO, HALO + cells_y)
    x_spans = ((0, HALO), inner_x, (inner_x[1], wide_x))
    y_spans = ((0, HALO), inner_y, (inner_y[1], wide_y))
    parts = (
        (ll_ref, xlo_ref, lh_ref),
        (ylo_ref, own_ref, yhi_ref),
        (hl_ref, xhi_ref, hh_ref),
    )
    gains = (1.0, 2.0, 4.0, 2.0)
    whole = slice(0, wide_y)
    zeros = jnp.zeros((HALO, cells_z), jnp.float32)
    tables = [table_ref[c] for c in range(4)]
    for i, (x0, x1) in enumerate(x_spans):
        for k, (y0, y1) in enumerate(y_spans):
            part = parts[i][k]
            inside = jnp.float32(1.0)
            if i != 1:
                inside = inside * where_ref[0, i // 2].astype(jnp.float32)
            if k != 1:
                inside = inside * where_ref[1, k // 2].astype(jnp.float32)

            def fill(x, carry, part=part, inside=inside, x0=x0, y0=y0, y1=y1):
                for comp in range(12):
                    even[comp, x0 + x, y0:y1, :] = part[comp, x] * gains[comp // 3]
                for y in range(y0, y1, 8):
                    ids = part[12, x, y - y0 : y - y0 + 8, :].astype(jnp.int32)
                    for c in range(4):
                        value = jnp.take_along_axis(tables[c], ids, axis=1)
                        coef[c, x0 + x, y : y + 8, :] = value * inside if c == 3 else value
                return carry

            lax.fori_loop(0, x1 - x0, fill, 0, unroll=2)
    for buffer in (even, odd):
        for comp in (0, 2):
            for x in range(wide_x):
                buffer[comp, x, wide_y:, :] = zeros

    lane = lax.broadcasted_iota(jnp.int32, (wide_y, cells_z), 1)
    not_last = lane < cells_z - 1
    not_first = lane > 0
    x_edge = where_ref[0, 0].astype(jnp.float32)
    y_edge = where_ref[1, 0].astype(jnp.float32)
    plane = HALO + where_ref[2, 0]

    def z_next(v):
        return jnp.where(not_last, pltpu.roll(v, cells_z - 1, 1), 0.0)

    def z_prev(v):
        return jnp.where(not_first, pltpu.roll(v, 1, 1), 0.0)

    def y_prev(v):
        return pltpu.roll(jnp.concatenate([v[:HALO] * y_edge, v[HALO:]], axis=0), 1, 0)

    for step in range(STEPS):
        old, new = (even, odd) if step % 2 == 0 else (odd, even)

        def magnetic(x, old=old):
            ex, ey, ez = (old[c, x, whole] for c in range(3))
            ey_x, ez_x = (old[1, x + 1, whole], old[2, x + 1, whole])
            ex_y, ez_y = (old[0, x, 1 : wide_y + 1], old[2, x, 1 : wide_y + 1])
            hx = old[3, x, whole] - ((ez_y - ez) - (z_next(ey) - ey))
            hy = old[4, x, whole] - ((z_next(ex) - ex) - (ez_x - ez))
            hz = old[5, x, whole] - ((ey_x - ey) - (ex_y - ex))
            return hx, hy, hz

        def electric(x, old=old, new=new):
            edge = jnp.where(x == HALO, x_edge, 1.0)
            hx, hy, hz = (new[3 + c, x, whole] for c in range(3))
            hy_x, hz_x = (new[c, x - 1, whole] * edge for c in (4, 5))
            curl = (
                (hz - y_prev(hz)) - (hy - z_prev(hy)),
                (hx - z_prev(hx)) - (hz - hz_x),
                (hy - hy_x) - (hx - y_prev(hx)),
            )
            keep, drive, coupled, scale = (coef[c, x] for c in range(4))
            for c in range(3):
                polar = old[6 + c, x, whole]
                field = old[c, x, whole]
                rate = keep * old[9 + c, x, whole] + drive * (coupled * field - polar)
                new[6 + c, x, whole] = polar + rate
                new[9 + c, x, whole] = rate
                new[c, x, whole] = field + scale * (curl[c] - rate)

        def put(x, values, new=new):
            for c in range(3):
                new[3 + c, x, whole] = values[c]

        def both(x, carry, magnetic=magnetic, electric=electric, put=put):
            after = magnetic(x + 1)
            electric(x)
            put(x + 1, after)
            return carry

        put(step, magnetic(step))
        put(step + 1, magnetic(step + 1))
        lax.fori_loop(step + 1, wide_x - 2 - step, both, 0)
        electric(wide_x - 2 - step)
        for slot, (comp, gain) in enumerate(((1, 1.0), (2, 1.0), (4, 0.5), (5, 0.5))):
            sample_out[step, slot] = new[comp, plane, inner_y[0] : inner_y[1], :] * gain

    final = even if STEPS % 2 == 0 else odd

    def emit(x, carry):
        for c in range(3):
            for base, out, gain in ((0, e_out, 1.0), (3, h_out, 0.5), (6, p_out, 0.25), (9, j_out, 0.5)):
                out[c, x] = final[base + c, HALO + x, inner_y[0] : inner_y[1], :] * gain
        return carry

    lax.fori_loop(0, cells_x, emit, 0, unroll=2)


def yee_steps(where, table, *blocks):
    cells = blocks[0].shape[1:]
    block = jax.ShapeDtypeStruct((3,) + cells, jnp.float32)
    wide = (cells[0] + 2 * HALO, cells[1] + 2 * HALO, cells[2])
    state = pltpu.VMEM((12, wide[0], wide[1] + 8, wide[2]), jnp.float32)
    return pl.pallas_call(
        yee_kernel,
        out_shape=[block] * 4 + [jax.ShapeDtypeStruct((STEPS, 4) + cells[1:], jnp.float32)],
        in_specs=[SMEM, VMEM] + [VMEM] * len(blocks),
        out_specs=[VMEM] * 5,
        scratch_shapes=[state, state, pltpu.VMEM((4,) + wide, jnp.float32)],
        compiler_params=pltpu.CompilerParams(vmem_limit_bytes=20 * 1024 * 1024),
        name="yee_steps",
    )(where, table, *blocks)


def halves(value):
    high = value.astype(jnp.bfloat16)
    return high, (value - high.astype(jnp.float32)).astype(jnp.bfloat16)


def phase_kernel(coarse_c, coarse_s, fine_c, fine_s, high_out, low_out):
    freqs, coarse, count = coarse_c.shape

    def one(f, carry):
        fc, fs = fine_c[f], fine_s[f]
        for a in range(coarse):
            cc, cs = coarse_c[f, a : a + 1], coarse_s[f, a : a + 1]
            rows = slice(a * FINE, (a + 1) * FINE)
            cos_high, cos_low = halves(cc * fc - cs * fs)
            sin_high, sin_low = halves(cs * fc + cc * fs)
            high_out[f, rows, :count] = cos_high
            high_out[f, rows, count:] = sin_high
            low_out[f, rows, :count] = cos_low
            low_out[f, rows, count:] = sin_low
        return carry

    lax.fori_loop(0, freqs, one, 0)


def z_phases(omegas, dir_z, cells_z):
    coarse = cells_z // FINE
    base = omegas[:, None, None] * (
        (FINE * jnp.arange(coarse)).astype(jnp.float32)[:, None] * dir_z[None, :]
    )
    fine = omegas[:, None, None] * (jnp.arange(FINE).astype(jnp.float32)[:, None] * dir_z[None, :])
    out = jax.ShapeDtypeStruct(
        (omegas.shape[0], cells_z, 2 * dir_z.shape[0]), jnp.bfloat16
    )
    return pl.pallas_call(
        phase_kernel,
        out_shape=[out, out],
        in_specs=[VMEM] * 4,
        out_specs=[VMEM] * 2,
        compiler_params=pltpu.CompilerParams(vmem_limit_bytes=8 * 1024 * 1024),
        cost_estimate=pl.CostEstimate(flops=8000000, bytes_accessed=3000000, transcendentals=0),
        name="z_phases",
    )(jnp.cos(base), jnp.sin(base), jnp.cos(fine), jnp.sin(fine))


def radiation_kernel(
    cos_ref, sin_ref, sample_ref, acc_ref, high_ref, low_ref, cosy_ref, siny_ref,
    dft_out, part_out, rows_ref,
):
    freqs, cells_y, _ = acc_ref.shape[1:]
    steps = sample_ref.shape[0]
    count = cosy_ref.shape[2]
    half = 4 * cells_y

    def one(f, carry):
        reals, imags = [], []
        for c in range(4):
            real = acc_ref[c, f]
            imag = acc_ref[4 + c, f]
            for n in range(steps):
                sample = sample_ref[n, c]
                real = real + cos_ref[n, f] * sample
                imag = imag - sin_ref[n, f] * sample
            dft_out[c, f] = real
            dft_out[4 + c, f] = imag
            reals.append(real)
            imags.append(imag)
        left_high, left_low = halves(jnp.concatenate(reals + imags, axis=0))
        high, low = high_ref[f], low_ref[f]

        def mul(a, b):
            return jnp.dot(a, b, preferred_element_type=jnp.float32)

        table = mul(left_high, high) + (mul(left_high, low) + mul(left_low, high))
        part_real = table[:half, :count] - table[half:, count:]
        part_imag = table[:half, count:] + table[half:, :count]
        cos_y, sin_y = cosy_ref[f], siny_ref[f]
        for c, (source, sign) in enumerate(((3, -1.0), (2, 1.0), (1, 1.0), (0, -1.0))):
            pr = part_real[source * cells_y : (source + 1) * cells_y]
            pi = part_imag[source * cells_y : (source + 1) * cells_y]
            out_real = jnp.sum(pr * cos_y - pi * sin_y, axis=0, keepdims=True)
            out_imag = jnp.sum(pr * sin_y + pi * cos_y, axis=0, keepdims=True)
            rows_ref[c, pl.ds(f, 1), :] = sign * out_real
            rows_ref[4 + c, pl.ds(f, 1), :] = sign * out_imag
        return carry

    lax.fori_loop(0, freqs, one, 0)
    half_count = count // 2
    rows = jnp.concatenate(
        [rows_ref[c, :, k * half_count : (k + 1) * half_count] for k in range(2) for c in range(8)],
        axis=0,
    )
    part_out[...] = rows.T


def radiate(cos_a, sin_a, samples, acc, high, low, cos_y, sin_y):
    count = cos_y.shape[2]
    freqs = acc.shape[1]
    return pl.pallas_call(
        radiation_kernel,
        out_shape=[
            jax.ShapeDtypeStruct(acc.shape, jnp.float32),
            jax.ShapeDtypeStruct((count // 2, 16 * freqs), jnp.float32),
        ],
        in_specs=[SMEM, SMEM] + [VMEM] * 6,
        out_specs=[VMEM] * 2,
        scratch_shapes=[pltpu.VMEM((8, freqs, count), jnp.float32)],
        compiler_params=pltpu.CompilerParams(vmem_limit_bytes=16 * 1024 * 1024),
        name="radiate",
    )(cos_a, sin_a, samples, acc, high, low, cos_y, sin_y)


def finish(arrived, scale, freqs):
    share = 2 * arrived.shape[1]

    def finish_kernel(in_ref, out_ref):
        total = jnp.sum(in_ref[...], axis=0) * scale
        half = total.shape[1] // 2
        both = jnp.concatenate([total, pltpu.roll(total, half, 1)], axis=0)
        out_ref[...] = both.T[:half].reshape(out_ref.shape)

    return pl.pallas_call(
        finish_kernel,
        out_shape=jax.ShapeDtypeStruct((8, freqs, share), jnp.float32),
        in_specs=[VMEM],
        out_specs=VMEM,
        compiler_params=pltpu.CompilerParams(vmem_limit_bytes=4 * 1024 * 1024),
        name="finish",
    )(arrived)


def spread_rows(samples, root):
    count = lax.axis_size("rows")
    pieces = samples.reshape(count, -1, samples.shape[-1])
    arrived = lax.all_to_all(pieces, "rows", split_axis=0, concat_axis=0, tiled=True)
    mine = lax.dynamic_index_in_dim(arrived, root, 0, keepdims=True)
    copies = jnp.broadcast_to(mine, pieces.shape)
    gathered = lax.all_to_all(copies, "rows", split_axis=0, concat_axis=0, tiled=True)
    return gathered.reshape(samples.shape)


def local(
    e_field, h_field, polar, polar_rate, material_id, eps_inf, delta_eps, pole_freq, damping,
    dft_acc, plane_index, direction_ids,
):
    cells_x, cells_y, cells_z = e_field.shape[1:]
    freq_block = dft_acc.shape[1]
    row, col = lax.axis_index("rows"), lax.axis_index("cols")
    rows, cols = lax.axis_size("rows"), lax.axis_size("cols")

    own, first, final = pack(e_field, h_field, polar, polar_rate, material_id)
    ylo = shifted(final, "cols", 1)
    yhi = shifted(first, "cols", -1)
    xhi = shifted(own, "rows", -1)
    xlo = shifted(own, "rows", 1)
    corner_hl = shifted(ylo, "rows", -1)
    corner_ll = shifted(ylo, "rows", 1)
    corner_hh = shifted(yhi, "rows", -1)
    corner_lh = shifted(yhi, "rows", 1)

    plane_row = plane_index[0]
    root_row = plane_row // cells_x
    local_row = plane_row % cells_x
    table = material_table(eps_inf, delta_eps, pole_freq, damping)
    where = jnp.stack(
        [row > 0, row < rows - 1, col > 0, col < cols - 1, local_row, local_row]
    ).astype(jnp.int32).reshape(3, 2)

    total_f = rows * freq_block
    freq_ids = row * freq_block + jnp.arange(freq_block, dtype=jnp.int32)
    omegas = OMEGA_LO + (OMEGA_HI - OMEGA_LO) * (freq_ids.astype(jnp.float32) / (total_f - 1))
    times = (jnp.arange(STEPS).astype(jnp.float32) + 1.0) * COURANT
    angles = times[:, None] * omegas[None, :]
    count = direction_ids.shape[0]
    share = count // cols
    pairs = direction_ids.reshape(cols, 2, share // 2, 2).transpose(1, 0, 2, 3)
    ids_float = pairs.reshape(count, 2).astype(jnp.float32)
    dir_y = SPREAD * (2.0 * ids_float[:, 0] / (G - 1) - 1.0)
    dir_z = SPREAD * (2.0 * ids_float[:, 1] / (G - 1) - 1.0)
    dir_x = jnp.sqrt(1.0 - dir_y * dir_y - dir_z * dir_z)
    pos_y = (col * cells_y + jnp.arange(cells_y, dtype=jnp.int32)).astype(jnp.float32)
    plane_x = plane_row.astype(jnp.float32)
    phase_y = (
        omegas[:, None, None] * (pos_y[:, None] * dir_y[None, :] + plane_x * dir_x[None, :])[None]
    )
    high, low = z_phases(omegas, dir_z, cells_z)
    waves = (
        jnp.cos(phase_y), jnp.sin(phase_y), jnp.cos(angles), jnp.sin(angles),
    )
    cos_y, sin_y, cos_a, sin_a = waves
    e_out, h_out, p_out, j_out, samples = yee_steps(
        where, table, own, ylo, yhi, xlo, xhi, corner_ll, corner_lh, corner_hl, corner_hh
    )
    received = spread_rows(samples, root_row)
    dft_out, partial_sum = radiate(
        cos_a, sin_a, received, dft_acc, high, low, cos_y, sin_y,
    )
    pieces = partial_sum.reshape(cols, -1, partial_sum.shape[-1])
    arrived = lax.all_to_all(pieces, "cols", split_axis=0, concat_axis=0, tiled=True)
    far_field = finish(arrived, 1.0 / math.sqrt(cols * cells_y * cells_z), freq_block)
    return (e_out, h_out, p_out, j_out, dft_out, far_field)


def solution(mesh):
    grid = P(None, "rows", "cols", None)
    in_specs = (
        grid, grid, grid, grid, P("rows", "cols", None), P(), P(), P(), P(), grid, P(), P(),
    )
    out_specs = (grid, grid, grid, grid, grid, P(None, "rows", "cols"))
    return jax.shard_map(local, mesh=mesh, in_specs=in_specs, out_specs=out_specs, check_vma=False)
```

```python
import math

import jax
import jax.numpy as jnp
from jax import lax
from jax.experimental import pallas as pl
from jax.experimental.pallas import tpu as pltpu
from jax.sharding import PartitionSpec as P


STEPS = 8
HALO = 8
G = 64
FINE = 16
LEVEL_BITS = 3

COURANT = 0.5
OMEGA_LO = 2.0 * math.pi / 24.0
OMEGA_HI = 2.0 * math.pi / 12.0
SPREAD = 0.7

VMEM = pl.BlockSpec(memory_space=pltpu.VMEM)
SMEM = pl.BlockSpec(memory_space=pltpu.SMEM)


def shifted(value, axis, steps):
    count = lax.axis_size(axis)
    first, last = (max(0, -steps), min(count, count - steps))
    return lax.ppermute(value, axis, [(source, source + steps) for source in range(first, last)])


def material_table(eps_inf, delta_eps, pole_freq, damping):
    half_damp = 0.5 * damping
    keep = (1.0 - half_damp) / (1.0 + half_damp)
    drive = pole_freq * pole_freq / COURANT / (1.0 + half_damp)
    return jnp.stack([keep, 0.5 * drive, 4.0 * delta_eps, 0.5 * (COURANT / eps_inf)])


def pack_kernel(e_ref, h_ref, p_ref, j_ref, m_ref, own, first, final, mats, sems):
    cells_y = e_ref.shape[2]
    spans = ((own, 0, cells_y), (first, 0, HALO), (final, cells_y - HALO, HALO))
    copies = [pltpu.make_async_copy(m_ref, mats, sems.at[0])]
    for i, ref in enumerate((e_ref, h_ref, p_ref, j_ref)):
        for k, (out, start, size) in enumerate(spans):
            copies.append(
                pltpu.make_async_copy(
                    ref.at[:, :, pl.ds(start, size), :],
                    out.at[pl.ds(3 * i, 3)],
                    sems.at[1 + 3 * i + k],
                )
            )
    for copy in copies:
        copy.start()
    copies[0].wait()
    ids = mats[...].astype(jnp.float32)
    own[12] = ids
    first[12] = ids[:, :HALO]
    final[12] = ids[:, cells_y - HALO :]
    for copy in copies[1:]:
        copy.wait()


def pack(e_field, h_field, polar, polar_rate, material_id):
    cells_x, cells_y, cells_z = material_id.shape
    strip = jax.ShapeDtypeStruct((13, cells_x, HALO, cells_z), jnp.float32)
    return pl.pallas_call(
        pack_kernel,
        out_shape=[
            jax.ShapeDtypeStruct((13, cells_x, cells_y, cells_z), jnp.float32), strip, strip,
        ],
        in_specs=[pl.BlockSpec(memory_space=pltpu.HBM)] * 5,
        out_specs=[VMEM] * 3,
        scratch_shapes=[
            pltpu.VMEM(material_id.shape, jnp.int32),
            pltpu.SemaphoreType.DMA((13,)),
        ],
        compiler_params=pltpu.CompilerParams(vmem_limit_bytes=8 * 1024 * 1024),
        name="pack",
    )(
        *(
            pltpu.with_memory_space_constraint(v, pltpu.HBM)
            for v in (e_field, h_field, polar, polar_rate, material_id)
        )
    )


def yee_kernel(
    where_ref, table_ref, own_ref, ylo_ref, yhi_ref, xlo_ref, xhi_ref, clo_ref, chi_ref,
    e_out, h_out, p_out, j_out, sample_out, even, odd, coef,
):
    cells_x, cells_y, cells_z = own_ref.shape[1:]
    wide_x = cells_x + 2 * HALO
    wide_y = cells_y + 2 * HALO
    inner_x, inner_y = (HALO, HALO + cells_x), (HALO, HALO + cells_y)
    x_spans = ((0, HALO), inner_x, (inner_x[1], wide_x))
    y_spans = ((0, HALO), inner_y, (inner_y[1], wide_y))
    parts = (
        (clo_ref.at[0], xlo_ref, clo_ref.at[1]),
        (ylo_ref, own_ref, yhi_ref),
        (chi_ref.at[0], xhi_ref, chi_ref.at[1]),
    )
    gains = (1.0, 2.0, 4.0, 2.0)
    whole = slice(0, wide_y)
    zeros = jnp.zeros((HALO, cells_z), jnp.float32)
    for i, (x0, x1) in enumerate(x_spans):
        for k, (y0, y1) in enumerate(y_spans):
            part = parts[i][k]
            inside = jnp.float32(1.0)
            if i != 1:
                inside = inside * where_ref[0, i // 2].astype(jnp.float32)
            if k != 1:
                inside = inside * where_ref[1, k // 2].astype(jnp.float32)

            def fill(x, carry, part=part, inside=inside, x0=x0, y0=y0, y1=y1):
                for comp in range(12):
                    even[comp, x0 + x, y0:y1, :] = part[comp, x] * gains[comp // 3]
                ids = part[12, x].astype(jnp.int32)
                bits = [(ids & (1 << k)) != 0 for k in range(LEVEL_BITS)]
                for c in range(4):
                    values = [table_ref[c, level] for level in range(1 << LEVEL_BITS)]
                    for bit in bits:
                        values = [
                            jnp.where(bit, odd_one, even_one)
                            for even_one, odd_one in zip(values[::2], values[1::2])
                        ]
                    value = values[0]
                    coef[c, x0 + x, y0:y1, :] = value * inside if c == 3 else value
                return carry

            lax.fori_loop(0, x1 - x0, fill, 0, unroll=8)
    for buffer in (even, odd):
        for comp in (0, 2):
            for x in range(wide_x):
                buffer[comp, x, wide_y:, :] = zeros

    lane = lax.broadcasted_iota(jnp.int32, (wide_y, cells_z), 1)
    not_last = lane < cells_z - 1
    not_first = lane > 0
    x_edge = where_ref[0, 0].astype(jnp.float32)
    y_edge = where_ref[1, 0].astype(jnp.float32)
    plane = HALO + where_ref[2, 0]

    def z_next(v):
        return jnp.where(not_last, pltpu.roll(v, cells_z - 1, 1), 0.0)

    def z_prev(v):
        return jnp.where(not_first, pltpu.roll(v, 1, 1), 0.0)

    def y_prev(v):
        return pltpu.roll(jnp.concatenate([v[:HALO] * y_edge, v[HALO:]], axis=0), 1, 0)

    for step in range(STEPS):
        old, new = (even, odd) if step % 2 == 0 else (odd, even)

        def magnetic(x, old=old):
            ex, ey, ez = (old[c, x, whole] for c in range(3))
            ey_x, ez_x = (old[1, x + 1, whole], old[2, x + 1, whole])
            ex_y, ez_y = (old[0, x, 1 : wide_y + 1], old[2, x, 1 : wide_y + 1])
            hx = old[3, x, whole] - ((ez_y - ez) - (z_next(ey) - ey))
            hy = old[4, x, whole] - ((z_next(ex) - ex) - (ez_x - ez))
            hz = old[5, x, whole] - ((ey_x - ey) - (ex_y - ex))
            return hx, hy, hz

        def electric(x, old=old, new=new):
            edge = jnp.where(x == HALO, x_edge, 1.0)
            hx, hy, hz = (new[3 + c, x, whole] for c in range(3))
            hy_x, hz_x = (new[c, x - 1, whole] * edge for c in (4, 5))
            curl = (
                (hz - y_prev(hz)) - (hy - z_prev(hy)),
                (hx - z_prev(hx)) - (hz - hz_x),
                (hy - hy_x) - (hx - y_prev(hx)),
            )
            keep, drive, coupled, scale = (coef[c, x] for c in range(4))
            for c in range(3):
                polar = old[6 + c, x, whole]
                field = old[c, x, whole]
                rate = keep * old[9 + c, x, whole] + drive * (coupled * field - polar)
                new[6 + c, x, whole] = polar + rate
                new[9 + c, x, whole] = rate
                new[c, x, whole] = field + scale * (curl[c] - rate)

        def put(x, values, new=new):
            for c in range(3):
                new[3 + c, x, whole] = values[c]

        def both(x, carry, magnetic=magnetic, electric=electric, put=put):
            after = magnetic(x + 1)
            electric(x)
            put(x + 1, after)
            return carry

        put(step, magnetic(step))
        put(step + 1, magnetic(step + 1))
        both(step + 1, 0)
        lax.fori_loop(step + 2, wide_x - 2 - step, both, 0, unroll=4)
        electric(wide_x - 2 - step)
        for slot, (comp, gain) in enumerate(((1, 1.0), (2, 1.0), (4, 0.5), (5, 0.5))):
            sample_out[step, slot] = new[comp, plane, inner_y[0] : inner_y[1], :] * gain

    final = even if STEPS % 2 == 0 else odd

    def emit(x, carry):
        for c in range(3):
            for base, out, gain in ((0, e_out, 1.0), (3, h_out, 0.5), (6, p_out, 0.25), (9, j_out, 0.5)):
                out[c, x] = final[base + c, HALO + x, inner_y[0] : inner_y[1], :] * gain
        return carry

    lax.fori_loop(0, cells_x, emit, 0, unroll=2)


def yee_steps(where, table, *blocks):
    cells = blocks[0].shape[1:]
    block = jax.ShapeDtypeStruct((3,) + cells, jnp.float32)
    wide = (cells[0] + 2 * HALO, cells[1] + 2 * HALO, cells[2])
    state = pltpu.VMEM((12, wide[0], wide[1] + 8, wide[2]), jnp.float32)
    return pl.pallas_call(
        yee_kernel,
        out_shape=[block] * 4 + [jax.ShapeDtypeStruct((STEPS, 4) + cells[1:], jnp.float32)],
        in_specs=[SMEM, SMEM] + [VMEM] * len(blocks),
        out_specs=[VMEM] * 5,
        scratch_shapes=[state, state, pltpu.VMEM((4,) + wide, jnp.float32)],
        compiler_params=pltpu.CompilerParams(vmem_limit_bytes=20 * 1024 * 1024),
        name="yee_steps",
    )(where, table, *blocks)


def halves(value):
    high = value.astype(jnp.bfloat16)
    return high, (value - high.astype(jnp.float32)).astype(jnp.bfloat16)


def phase_kernel(coarse_c, coarse_s, fine_c, fine_s, high_out, low_out):
    freqs, coarse, count = coarse_c.shape

    def one(f, carry):
        fc, fs = fine_c[f], fine_s[f]
        for a in range(coarse):
            cc, cs = coarse_c[f, a : a + 1], coarse_s[f, a : a + 1]
            rows = slice(a * FINE, (a + 1) * FINE)
            cos_high, cos_low = halves(cc * fc - cs * fs)
            sin_high, sin_low = halves(cs * fc + cc * fs)
            high_out[f, rows, :count] = cos_high
            high_out[f, rows, count:] = sin_high
            low_out[f, rows, :count] = cos_low
            low_out[f, rows, count:] = sin_low
        return carry

    lax.fori_loop(0, freqs, one, 0)


def z_phases(omegas, dir_z, cells_z):
    coarse = cells_z // FINE
    base = omegas[:, None, None] * (
        (FINE * jnp.arange(coarse)).astype(jnp.float32)[:, None] * dir_z[None, :]
    )
    fine = omegas[:, None, None] * (jnp.arange(FINE).astype(jnp.float32)[:, None] * dir_z[None, :])
    out = jax.ShapeDtypeStruct(
        (omegas.shape[0], cells_z, 2 * dir_z.shape[0]), jnp.bfloat16
    )
    return pl.pallas_call(
        phase_kernel,
        out_shape=[out, out],
        in_specs=[VMEM] * 4,
        out_specs=[VMEM] * 2,
        compiler_params=pltpu.CompilerParams(vmem_limit_bytes=8 * 1024 * 1024),
        cost_estimate=pl.CostEstimate(flops=8000000, bytes_accessed=3000000, transcendentals=0),
        name="z_phases",
    )(jnp.cos(base), jnp.sin(base), jnp.cos(fine), jnp.sin(fine))


def radiation_kernel(
    cos_ref, sin_ref, sample_ref, acc_ref, high_ref, low_ref, cosy_ref, siny_ref,
    dft_out, part_out, rows_ref,
):
    freqs, cells_y, _ = acc_ref.shape[1:]
    steps = sample_ref.shape[0]
    count = cosy_ref.shape[2]
    half = 4 * cells_y

    def one(f, carry):
        reals, imags = [], []
        for c in range(4):
            real = acc_ref[c, f]
            imag = acc_ref[4 + c, f]
            for n in range(steps):
                sample = sample_ref[n, c]
                real = real + cos_ref[n, f] * sample
                imag = imag - sin_ref[n, f] * sample
            dft_out[c, f] = real
            dft_out[4 + c, f] = imag
            reals.append(real)
            imags.append(imag)
        left_high, left_low = halves(jnp.concatenate(reals + imags, axis=0))
        high, low = high_ref[f], low_ref[f]

        def mul(a, b):
            return jnp.dot(a, b, preferred_element_type=jnp.float32)

        table = mul(
            jnp.concatenate([left_high, left_low], axis=1), jnp.concatenate([high, high], axis=0)
        ) + mul(left_high, low)
        part_real = table[:half, :count] - table[half:, count:]
        part_imag = table[:half, count:] + table[half:, :count]
        cos_y, sin_y = cosy_ref[f], siny_ref[f]
        for c, (source, sign) in enumerate(((3, -1.0), (2, 1.0), (1, 1.0), (0, -1.0))):
            pr = part_real[source * cells_y : (source + 1) * cells_y]
            pi = part_imag[source * cells_y : (source + 1) * cells_y]
            out_real = jnp.sum(pr * cos_y - pi * sin_y, axis=0, keepdims=True)
            out_imag = jnp.sum(pr * sin_y + pi * cos_y, axis=0, keepdims=True)
            rows_ref[c, pl.ds(f, 1), :] = sign * out_real
            rows_ref[4 + c, pl.ds(f, 1), :] = sign * out_imag
        return carry

    lax.fori_loop(0, freqs, one, 0, unroll=8)
    half_count = count // 2
    rows = jnp.concatenate(
        [rows_ref[c, :, k * half_count : (k + 1) * half_count] for k in range(2) for c in range(8)],
        axis=0,
    )
    part_out[...] = rows.T


def radiate(cos_a, sin_a, samples, acc, high, low, cos_y, sin_y):
    count = cos_y.shape[2]
    freqs = acc.shape[1]
    return pl.pallas_call(
        radiation_kernel,
        out_shape=[
            jax.ShapeDtypeStruct(acc.shape, jnp.float32),
            jax.ShapeDtypeStruct((count // 2, 16 * freqs), jnp.float32),
        ],
        in_specs=[SMEM, SMEM] + [VMEM] * 6,
        out_specs=[VMEM] * 2,
        scratch_shapes=[pltpu.VMEM((8, freqs, count), jnp.float32)],
        compiler_params=pltpu.CompilerParams(vmem_limit_bytes=16 * 1024 * 1024),
        name="radiate",
    )(cos_a, sin_a, samples, acc, high, low, cos_y, sin_y)


def finish(arrived, scale, freqs):
    share = 2 * arrived.shape[1]

    def finish_kernel(in_ref, out_ref):
        total = jnp.sum(in_ref[...], axis=0) * scale
        half = total.shape[1] // 2
        both = jnp.concatenate([total, pltpu.roll(total, half, 1)], axis=0)
        out_ref[...] = both.T[:half].reshape(out_ref.shape)

    return pl.pallas_call(
        finish_kernel,
        out_shape=jax.ShapeDtypeStruct((8, freqs, share), jnp.float32),
        in_specs=[VMEM],
        out_specs=VMEM,
        compiler_params=pltpu.CompilerParams(vmem_limit_bytes=4 * 1024 * 1024),
        name="finish",
    )(arrived)


def spread_rows(samples, root):
    count = lax.axis_size("rows")
    pieces = samples.reshape(count, -1, samples.shape[-1])
    arrived = lax.all_to_all(pieces, "rows", split_axis=0, concat_axis=0, tiled=True)
    mine = lax.dynamic_index_in_dim(arrived, root, 0, keepdims=True)
    copies = jnp.broadcast_to(mine, pieces.shape)
    gathered = lax.all_to_all(copies, "rows", split_axis=0, concat_axis=0, tiled=True)
    return gathered.reshape(samples.shape)


def local(
    e_field, h_field, polar, polar_rate, material_id, eps_inf, delta_eps, pole_freq, damping,
    dft_acc, plane_index, direction_ids,
):
    cells_x, cells_y, cells_z = e_field.shape[1:]
    freq_block = dft_acc.shape[1]
    row, col = lax.axis_index("rows"), lax.axis_index("cols")
    rows, cols = lax.axis_size("rows"), lax.axis_size("cols")

    own, first, final = pack(e_field, h_field, polar, polar_rate, material_id)
    yhi = shifted(first, "cols", -1)
    ylo = shifted(final, "cols", 1)
    xhi = shifted(own, "rows", -1)
    xlo = shifted(own, "rows", 1)
    sides = jnp.stack([ylo, yhi])
    chi = shifted(sides, "rows", -1)
    clo = shifted(sides, "rows", 1)

    plane_row = plane_index[0]
    root_row = plane_row // cells_x
    local_row = plane_row % cells_x
    table = material_table(eps_inf, delta_eps, pole_freq, damping)
    where = jnp.stack(
        [row > 0, row < rows - 1, col > 0, col < cols - 1, local_row, local_row]
    ).astype(jnp.int32).reshape(3, 2)

    total_f = rows * freq_block
    freq_ids = row * freq_block + jnp.arange(freq_block, dtype=jnp.int32)
    omegas = OMEGA_LO + (OMEGA_HI - OMEGA_LO) * (freq_ids.astype(jnp.float32) / (total_f - 1))
    times = (jnp.arange(STEPS).astype(jnp.float32) + 1.0) * COURANT
    angles = times[:, None] * omegas[None, :]
    count = direction_ids.shape[0]
    share = count // cols
    pairs = direction_ids.reshape(cols, 2, share // 2, 2).transpose(1, 0, 2, 3)
    ids_float = pairs.reshape(count, 2).astype(jnp.float32)
    dir_y = SPREAD * (2.0 * ids_float[:, 0] / (G - 1) - 1.0)
    dir_z = SPREAD * (2.0 * ids_float[:, 1] / (G - 1) - 1.0)
    dir_x = jnp.sqrt(1.0 - dir_y * dir_y - dir_z * dir_z)
    pos_y = (col * cells_y + jnp.arange(cells_y, dtype=jnp.int32)).astype(jnp.float32)
    plane_x = plane_row.astype(jnp.float32)
    phase_y = (
        omegas[:, None, None] * (pos_y[:, None] * dir_y[None, :] + plane_x * dir_x[None, :])[None]
    )
    high, low = z_phases(omegas, dir_z, cells_z)
    waves = (
        jnp.cos(phase_y), jnp.sin(phase_y), jnp.cos(angles), jnp.sin(angles),
    )
    cos_y, sin_y, cos_a, sin_a = waves
    e_out, h_out, p_out, j_out, samples = yee_steps(
        where, table, own, ylo, yhi, xlo, xhi, clo, chi
    )
    received = spread_rows(samples, root_row)
    dft_out, partial_sum = radiate(
        cos_a, sin_a, received, dft_acc, high, low, cos_y, sin_y,
    )
    pieces = partial_sum.reshape(cols, -1, partial_sum.shape[-1])
    arrived = lax.all_to_all(pieces, "cols", split_axis=0, concat_axis=0, tiled=True)
    far_field = finish(arrived, 1.0 / math.sqrt(cols * cells_y * cells_z), freq_block)
    return (e_out, h_out, p_out, j_out, dft_out, far_field)


def solution(mesh):
    grid = P(None, "rows", "cols", None)
    in_specs = (
        grid, grid, grid, grid, P("rows", "cols", None), P(), P(), P(), P(), grid, P(), P(),
    )
    out_specs = (grid, grid, grid, grid, grid, P(None, "rows", "cols"))
    return jax.shard_map(local, mesh=mesh, in_specs=in_specs, out_specs=out_specs, check_vma=False)
```

```python
import math

import jax
import jax.numpy as jnp
from jax import lax
from jax.experimental import pallas as pl
from jax.experimental.pallas import tpu as pltpu
from jax.sharding import PartitionSpec as P


STEPS = 8
HALO = 8
G = 64
FINE = 16
LEVEL_BITS = 3

COURANT = 0.5
OMEGA_LO = 2.0 * math.pi / 24.0
OMEGA_HI = 2.0 * math.pi / 12.0
SPREAD = 0.7

VMEM = pl.BlockSpec(memory_space=pltpu.VMEM)
SMEM = pl.BlockSpec(memory_space=pltpu.SMEM)


def shifted(value, axis, steps):
    count = lax.axis_size(axis)
    first, last = (max(0, -steps), min(count, count - steps))
    return lax.ppermute(value, axis, [(source, source + steps) for source in range(first, last)])


def material_table(eps_inf, delta_eps, pole_freq, damping):
    half_damp = 0.5 * damping
    keep = (1.0 - half_damp) / (1.0 + half_damp)
    drive = pole_freq * pole_freq / COURANT / (1.0 + half_damp)
    return jnp.stack([keep, 0.5 * drive, 4.0 * delta_eps, 0.5 * (COURANT / eps_inf)])


def pack_kernel(e_ref, h_ref, p_ref, j_ref, m_ref, own, first, final, mats, sems):
    cells_y = e_ref.shape[2]
    copies = [
        pltpu.make_async_copy(ref, own.at[pl.ds(3 * i, 3)], sems.at[i])
        for i, ref in enumerate((e_ref, h_ref, p_ref, j_ref))
    ]
    copies.append(pltpu.make_async_copy(m_ref, mats, sems.at[4]))
    for copy in copies:
        copy.start()
    for i, copy in enumerate(copies):
        copy.wait()
        span = pl.ds(3 * i, 3) if i < 4 else pl.ds(12, 1)
        if i == 4:
            own[span] = mats[...].astype(jnp.float32)[None]
        first[span] = own[span, :, :HALO, :]
        final[span] = own[span, :, cells_y - HALO :, :]


def pack(e_field, h_field, polar, polar_rate, material_id):
    cells_x, cells_y, cells_z = material_id.shape
    strip = jax.ShapeDtypeStruct((13, cells_x, HALO, cells_z), jnp.float32)
    return pl.pallas_call(
        pack_kernel,
        out_shape=[
            jax.ShapeDtypeStruct((13, cells_x, cells_y, cells_z), jnp.float32), strip, strip,
        ],
        in_specs=[pl.BlockSpec(memory_space=pltpu.HBM)] * 5,
        out_specs=[VMEM] * 3,
        scratch_shapes=[
            pltpu.VMEM(material_id.shape, jnp.int32),
            pltpu.SemaphoreType.DMA((5,)),
        ],
        compiler_params=pltpu.CompilerParams(vmem_limit_bytes=8 * 1024 * 1024),
        name="pack",
    )(
        *(
            pltpu.with_memory_space_constraint(v, pltpu.HBM)
            for v in (e_field, h_field, polar, polar_rate, material_id)
        )
    )


def yee_kernel(
    where_ref, table_ref, own_ref, ylo_ref, yhi_ref, xlo_ref, xhi_ref, clo_ref, chi_ref,
    e_out, h_out, p_out, j_out, sample_out, even, odd, coef,
):
    cells_x, cells_y, cells_z = own_ref.shape[1:]
    wide_x = cells_x + 2 * HALO
    wide_y = cells_y + 2 * HALO
    inner_x, inner_y = (HALO, HALO + cells_x), (HALO, HALO + cells_y)
    x_spans = ((0, HALO), inner_x, (inner_x[1], wide_x))
    y_spans = ((0, HALO), inner_y, (inner_y[1], wide_y))
    parts = (
        (clo_ref.at[0], xlo_ref, clo_ref.at[1]),
        (ylo_ref, own_ref, yhi_ref),
        (chi_ref.at[0], xhi_ref, chi_ref.at[1]),
    )
    gains = (1.0, 2.0, 4.0, 2.0)
    whole = slice(0, wide_y)
    zeros = jnp.zeros((HALO, cells_z), jnp.float32)
    for i, (x0, x1) in enumerate(x_spans):
        for k, (y0, y1) in enumerate(y_spans):
            part = parts[i][k]
            inside = jnp.float32(1.0)
            if i != 1:
                inside = inside * where_ref[0, i // 2].astype(jnp.float32)
            if k != 1:
                inside = inside * where_ref[1, k // 2].astype(jnp.float32)

            def fill(x, carry, part=part, inside=inside, x0=x0, y0=y0, y1=y1):
                for comp in range(12):
                    even[comp, x0 + x, y0:y1, :] = part[comp, x] * gains[comp // 3]
                ids = part[12, x].astype(jnp.int32)
                bits = [(ids & (1 << k)) != 0 for k in range(LEVEL_BITS)]
                for c in range(4):
                    values = [table_ref[c, level] for level in range(1 << LEVEL_BITS)]
                    for bit in bits:
                        values = [
                            jnp.where(bit, odd_one, even_one)
                            for even_one, odd_one in zip(values[::2], values[1::2])
                        ]
                    value = values[0]
                    coef[c, x0 + x, y0:y1, :] = value * inside if c == 3 else value
                return carry

            lax.fori_loop(0, x1 - x0, fill, 0, unroll=8)
    for buffer in (even, odd):
        for comp in (0, 2):
            for x in range(wide_x):
                buffer[comp, x, wide_y:, :] = zeros

    lane = lax.broadcasted_iota(jnp.int32, (wide_y, cells_z), 1)
    not_last = lane < cells_z - 1
    not_first = lane > 0
    x_edge = where_ref[0, 0].astype(jnp.float32)
    y_edge = where_ref[1, 0].astype(jnp.float32)
    plane = HALO + where_ref[2, 0]

    def z_next(v):
        return jnp.where(not_last, pltpu.roll(v, cells_z - 1, 1), 0.0)

    def z_prev(v):
        return jnp.where(not_first, pltpu.roll(v, 1, 1), 0.0)

    def y_prev(v):
        return pltpu.roll(jnp.concatenate([v[:HALO] * y_edge, v[HALO:]], axis=0), 1, 0)

    for step in range(STEPS):
        old, new = (even, odd) if step % 2 == 0 else (odd, even)

        def magnetic(x, old=old):
            ex, ey, ez = (old[c, x, whole] for c in range(3))
            ey_x, ez_x = (old[1, x + 1, whole], old[2, x + 1, whole])
            ex_y, ez_y = (old[0, x, 1 : wide_y + 1], old[2, x, 1 : wide_y + 1])
            hx = old[3, x, whole] - ((ez_y - ez) - (z_next(ey) - ey))
            hy = old[4, x, whole] - ((z_next(ex) - ex) - (ez_x - ez))
            hz = old[5, x, whole] - ((ey_x - ey) - (ex_y - ex))
            return hx, hy, hz

        def electric(x, old=old, new=new):
            edge = jnp.where(x == HALO, x_edge, 1.0)
            hx, hy, hz = (new[3 + c, x, whole] for c in range(3))
            hy_x, hz_x = (new[c, x - 1, whole] * edge for c in (4, 5))
            curl = (
                (hz - y_prev(hz)) - (hy - z_prev(hy)),
                (hx - z_prev(hx)) - (hz - hz_x),
                (hy - hy_x) - (hx - y_prev(hx)),
            )
            keep, drive, coupled, scale = (coef[c, x] for c in range(4))
            for c in range(3):
                polar = old[6 + c, x, whole]
                field = old[c, x, whole]
                rate = keep * old[9 + c, x, whole] + drive * (coupled * field - polar)
                new[6 + c, x, whole] = polar + rate
                new[9 + c, x, whole] = rate
                new[c, x, whole] = field + scale * (curl[c] - rate)

        def put(x, values, new=new):
            for c in range(3):
                new[3 + c, x, whole] = values[c]

        def both(x, carry, magnetic=magnetic, electric=electric, put=put):
            after = magnetic(x + 1)
            electric(x)
            put(x + 1, after)
            return carry

        put(step, magnetic(step))
        put(step + 1, magnetic(step + 1))
        both(step + 1, 0)
        lax.fori_loop(step + 2, wide_x - 2 - step, both, 0, unroll=4)
        electric(wide_x - 2 - step)
        for slot, (comp, gain) in enumerate(((1, 1.0), (2, 1.0), (4, 0.5), (5, 0.5))):
            sample_out[step, slot] = new[comp, plane, inner_y[0] : inner_y[1], :] * gain

    final = even if STEPS % 2 == 0 else odd

    def emit(x, carry):
        for c in range(3):
            for base, out, gain in ((0, e_out, 1.0), (3, h_out, 0.5), (6, p_out, 0.25), (9, j_out, 0.5)):
                out[c, x] = final[base + c, HALO + x, inner_y[0] : inner_y[1], :] * gain
        return carry

    lax.fori_loop(0, cells_x, emit, 0, unroll=2)


def yee_steps(where, table, *blocks):
    cells = blocks[0].shape[1:]
    block = jax.ShapeDtypeStruct((3,) + cells, jnp.float32)
    wide = (cells[0] + 2 * HALO, cells[1] + 2 * HALO, cells[2])
    state = pltpu.VMEM((12, wide[0], wide[1] + 8, wide[2]), jnp.float32)
    return pl.pallas_call(
        yee_kernel,
        out_shape=[block] * 4 + [jax.ShapeDtypeStruct((STEPS, 4) + cells[1:], jnp.float32)],
        in_specs=[SMEM, SMEM] + [VMEM] * len(blocks),
        out_specs=[VMEM] * 5,
        scratch_shapes=[state, state, pltpu.VMEM((4,) + wide, jnp.float32)],
        compiler_params=pltpu.CompilerParams(vmem_limit_bytes=20 * 1024 * 1024),
        name="yee_steps",
    )(where, table, *blocks)


def halves(value):
    high = value.astype(jnp.bfloat16)
    return high, (value - high.astype(jnp.float32)).astype(jnp.bfloat16)


def phase_kernel(coarse_c, coarse_s, fine_c, fine_s, high_out, low_out):
    freqs, coarse, count = coarse_c.shape

    def one(f, carry):
        fc, fs = fine_c[f], fine_s[f]
        for a in range(coarse):
            cc, cs = coarse_c[f, a : a + 1], coarse_s[f, a : a + 1]
            rows = slice(a * FINE, (a + 1) * FINE)
            cos_high, cos_low = halves(cc * fc - cs * fs)
            sin_high, sin_low = halves(cs * fc + cc * fs)
            high_out[f, rows, :count] = cos_high
            high_out[f, rows, count:] = sin_high
            low_out[f, rows, :count] = cos_low
            low_out[f, rows, count:] = sin_low
        return carry

    lax.fori_loop(0, freqs, one, 0)


def z_phases(omegas, dir_z, cells_z):
    coarse = cells_z // FINE
    base = omegas[:, None, None] * (
        (FINE * jnp.arange(coarse)).astype(jnp.float32)[:, None] * dir_z[None, :]
    )
    fine = omegas[:, None, None] * (jnp.arange(FINE).astype(jnp.float32)[:, None] * dir_z[None, :])
    out = jax.ShapeDtypeStruct(
        (omegas.shape[0], cells_z, 2 * dir_z.shape[0]), jnp.bfloat16
    )
    return pl.pallas_call(
        phase_kernel,
        out_shape=[out, out],
        in_specs=[VMEM] * 4,
        out_specs=[VMEM] * 2,
        compiler_params=pltpu.CompilerParams(vmem_limit_bytes=8 * 1024 * 1024),
        cost_estimate=pl.CostEstimate(flops=8000000, bytes_accessed=3000000, transcendentals=0),
        name="z_phases",
    )(jnp.cos(base), jnp.sin(base), jnp.cos(fine), jnp.sin(fine))


def radiation_kernel(
    cos_ref, sin_ref, sample_ref, acc_ref, high_ref, low_ref, cosy_ref, siny_ref,
    dft_out, part_out, rows_ref,
):
    freqs, cells_y, _ = acc_ref.shape[1:]
    steps = sample_ref.shape[0]
    count = cosy_ref.shape[2]
    half = 4 * cells_y

    def one(f, carry):
        reals, imags = [], []
        for c in range(4):
            real = acc_ref[c, f]
            imag = acc_ref[4 + c, f]
            for n in range(steps):
                sample = sample_ref[n, c]
                real = real + cos_ref[n, f] * sample
                imag = imag - sin_ref[n, f] * sample
            dft_out[c, f] = real
            dft_out[4 + c, f] = imag
            reals.append(real)
            imags.append(imag)
        left_high, left_low = halves(jnp.concatenate(reals + imags, axis=0))
        high, low = high_ref[f], low_ref[f]

        def mul(a, b):
            return jnp.dot(a, b, preferred_element_type=jnp.float32)

        table = mul(
            jnp.concatenate([left_high, left_low], axis=1), jnp.concatenate([high, high], axis=0)
        ) + mul(left_high, low)
        part_real = table[:half, :count] - table[half:, count:]
        part_imag = table[:half, count:] + table[half:, :count]
        cos_y, sin_y = cosy_ref[f], siny_ref[f]
        for c, (source, sign) in enumerate(((3, -1.0), (2, 1.0), (1, 1.0), (0, -1.0))):
            pr = part_real[source * cells_y : (source + 1) * cells_y]
            pi = part_imag[source * cells_y : (source + 1) * cells_y]
            out_real = jnp.sum(pr * cos_y - pi * sin_y, axis=0, keepdims=True)
            out_imag = jnp.sum(pr * sin_y + pi * cos_y, axis=0, keepdims=True)
            rows_ref[c, pl.ds(f, 1), :] = sign * out_real
            rows_ref[4 + c, pl.ds(f, 1), :] = sign * out_imag
        return carry

    lax.fori_loop(0, freqs, one, 0, unroll=8)
    half_count = count // 2
    rows = jnp.concatenate(
        [rows_ref[c, :, k * half_count : (k + 1) * half_count] for k in range(2) for c in range(8)],
        axis=0,
    )
    part_out[...] = rows.T


def radiate(cos_a, sin_a, samples, acc, high, low, cos_y, sin_y):
    count = cos_y.shape[2]
    freqs = acc.shape[1]
    return pl.pallas_call(
        radiation_kernel,
        out_shape=[
            jax.ShapeDtypeStruct(acc.shape, jnp.float32),
            jax.ShapeDtypeStruct((count // 2, 16 * freqs), jnp.float32),
        ],
        in_specs=[SMEM, SMEM] + [VMEM] * 6,
        out_specs=[VMEM] * 2,
        scratch_shapes=[pltpu.VMEM((8, freqs, count), jnp.float32)],
        compiler_params=pltpu.CompilerParams(vmem_limit_bytes=16 * 1024 * 1024),
        name="radiate",
    )(cos_a, sin_a, samples, acc, high, low, cos_y, sin_y)


def finish(arrived, scale, freqs):
    share = 2 * arrived.shape[1]

    def finish_kernel(in_ref, out_ref):
        total = jnp.sum(in_ref[...], axis=0) * scale
        half = total.shape[1] // 2
        both = jnp.concatenate([total, pltpu.roll(total, half, 1)], axis=0)
        out_ref[...] = both.T[:half].reshape(out_ref.shape)

    return pl.pallas_call(
        finish_kernel,
        out_shape=jax.ShapeDtypeStruct((8, freqs, share), jnp.float32),
        in_specs=[VMEM],
        out_specs=VMEM,
        compiler_params=pltpu.CompilerParams(vmem_limit_bytes=4 * 1024 * 1024),
        name="finish",
    )(arrived)


def spread_rows(samples, root, beside):
    count = lax.axis_size("rows")
    pieces = samples.reshape(count, -1, samples.shape[-1])
    arrived = lax.all_to_all(pieces, "rows", split_axis=0, concat_axis=0, tiled=True)
    mine = lax.dynamic_index_in_dim(arrived, root, 0, keepdims=True)
    mine, beside = lax.optimization_barrier((mine, beside))
    copies = jnp.broadcast_to(mine, pieces.shape)
    gathered = lax.all_to_all(copies, "rows", split_axis=0, concat_axis=0, tiled=True)
    return gathered.reshape(samples.shape), beside


def local(
    e_field, h_field, polar, polar_rate, material_id, eps_inf, delta_eps, pole_freq, damping,
    dft_acc, plane_index, direction_ids,
):
    cells_x, cells_y, cells_z = e_field.shape[1:]
    freq_block = dft_acc.shape[1]
    row, col = lax.axis_index("rows"), lax.axis_index("cols")
    rows, cols = lax.axis_size("rows"), lax.axis_size("cols")

    own, first, final = pack(e_field, h_field, polar, polar_rate, material_id)
    yhi = shifted(first, "cols", -1)
    ylo = shifted(final, "cols", 1)
    xhi = shifted(own, "rows", -1)
    xlo = shifted(own, "rows", 1)
    sides = jnp.stack([ylo, yhi])
    chi = shifted(sides, "rows", -1)
    clo = shifted(sides, "rows", 1)

    plane_row = plane_index[0]
    root_row = plane_row // cells_x
    local_row = plane_row % cells_x
    table = material_table(eps_inf, delta_eps, pole_freq, damping)
    where = jnp.stack(
        [row > 0, row < rows - 1, col > 0, col < cols - 1, local_row, local_row]
    ).astype(jnp.int32).reshape(3, 2)

    total_f = rows * freq_block
    freq_ids = row * freq_block + jnp.arange(freq_block, dtype=jnp.int32)
    omegas = OMEGA_LO + (OMEGA_HI - OMEGA_LO) * (freq_ids.astype(jnp.float32) / (total_f - 1))
    times = (jnp.arange(STEPS).astype(jnp.float32) + 1.0) * COURANT
    angles = times[:, None] * omegas[None, :]
    count = direction_ids.shape[0]
    share = count // cols
    pairs = direction_ids.reshape(cols, 2, share // 2, 2).transpose(1, 0, 2, 3)
    ids_float = pairs.reshape(count, 2).astype(jnp.float32)
    dir_y = SPREAD * (2.0 * ids_float[:, 0] / (G - 1) - 1.0)
    dir_z = SPREAD * (2.0 * ids_float[:, 1] / (G - 1) - 1.0)
    dir_x = jnp.sqrt(1.0 - dir_y * dir_y - dir_z * dir_z)
    pos_y = (col * cells_y + jnp.arange(cells_y, dtype=jnp.int32)).astype(jnp.float32)
    plane_x = plane_row.astype(jnp.float32)
    e_out, h_out, p_out, j_out, samples = yee_steps(
        where, table, own, ylo, yhi, xlo, xhi, clo, chi
    )
    samples, pos_y, omegas, dir_x, dir_y, dir_z, angles = lax.optimization_barrier(
        (samples, pos_y, omegas, dir_x, dir_y, dir_z, angles)
    )
    phase_y = (
        omegas[:, None, None] * (pos_y[:, None] * dir_y[None, :] + plane_x * dir_x[None, :])[None]
    )
    high, low = z_phases(omegas, dir_z, cells_z)
    waves = (
        high, low, jnp.cos(phase_y), jnp.sin(phase_y), jnp.cos(angles), jnp.sin(angles),
    )
    received, waves = spread_rows(samples, root_row, waves)
    high, low, cos_y, sin_y, cos_a, sin_a = waves
    dft_out, partial_sum = radiate(
        cos_a, sin_a, received, dft_acc, high, low, cos_y, sin_y,
    )
    pieces = partial_sum.reshape(cols, -1, partial_sum.shape[-1])
    arrived = lax.all_to_all(pieces, "cols", split_axis=0, concat_axis=0, tiled=True)
    far_field = finish(arrived, 1.0 / math.sqrt(cols * cells_y * cells_z), freq_block)
    return (e_out, h_out, p_out, j_out, dft_out, far_field)


def solution(mesh):
    grid = P(None, "rows", "cols", None)
    in_specs = (
        grid, grid, grid, grid, P("rows", "cols", None), P(), P(), P(), P(), grid, P(), P(),
    )
    out_specs = (grid, grid, grid, grid, grid, P(None, "rows", "cols"))
    return jax.shard_map(local, mesh=mesh, in_specs=in_specs, out_specs=out_specs, check_vma=False)
```
